512 devices in a mesh: seq: 16 (over x_hi, y), fsdp: 16 (over z, core), dp: 2 (over x_lo).
Axes of the slice: x: 4 (x_hi: 2, x_lo: 2; x = x_hi * 2 + x_lo), y: 8, z: 8, core: 2. Of those that a mesh axis runs over, the one named last changes fastest.
Arguments:
- query_rows: bfloat16 [16, 2048, 2048], P('fsdp', 'seq', 'dp'), may hold values from -32 to 32
- key_rows: bfloat16 [16, 2048, 2048], P('fsdp', 'seq', 'dp'), may hold values from -32 to 32
- value_rows: bfloat16 [16, 2048, 2048], P('fsdp', 'seq', 'dp'), may hold values from -6 to 6
- summary_keys: bfloat16 [16, 128, 2048], P('fsdp', 'seq', 'dp'), may hold values from -6 to 6
- summary_values: bfloat16 [16, 128, 2048], P('fsdp', 'seq', 'dp'), may hold values from -6 to 6
- out_grad: bfloat16 [16, 2048, 2048], P('fsdp', 'seq', 'dp'), may hold values from -6 to 6
- rel_bias: float32 [4, 16], P(None, 'fsdp'), may hold values from -2 to 2
- pattern: int32 [16, 16, 3], P('fsdp'), may hold values from -1 to 15, as said below
- block_view: int32 [16, 16], P('fsdp'), may hold values from 0 to 95, as said below
- summary_view: int32 [16, 128], P('fsdp'), may hold values from 0 to 95
Outputs:
- attended: bfloat16 [16, 2048, 2048], P('fsdp', 'seq', 'dp')
- query_grad: bfloat16 [16, 2048, 2048], P('fsdp', 'seq', 'dp')
- key_grad: bfloat16 [16, 2048, 2048], P('fsdp', 'seq', 'dp')
- value_grad: bfloat16 [16, 2048, 2048], P('fsdp', 'seq', 'dp')
- summary_key_grad: bfloat16 [16, 128, 2048], P('fsdp', 'seq', 'dp')
- summary_value_grad: bfloat16 [16, 128, 2048], P('fsdp', 'seq', 'dp')
- bias_grad: float32 [4, 16], P(None, 'fsdp')
The draws below stay inside these ranges and needn't reach their ends.
Inputs may be any that keep to these rules, and one draw needn't show every extreme that they name: `pattern`: slot j of block b's list holds b + j - 1 or -1 (no block); slot 1 always holds b. `block_view`: blocks that follow each other have equal views or views one apart on the cycle of 96 views.
All inputs are finite; a program needn't handle non-finite values.
Results may differ from the reference program's by a relative error of at most 0.0074.
Values may be sent and summed in bfloat16 or wider, within the bound.
No kernel may reach another device: no remote copies, remote signals or barrier semaphores. Data moves between devices by JAX's collectives and lax.ppermute only.
A program may use at most 64 MiB of HBM per device.

```python
import functools
import math
import jax
import jax.numpy as jnp
from jax import lax

HEADS = 16
HSIZE = 128
BLK = 128
NVIEW = 96
NREL = 4
SAMPLES = 16
TOKENS = 2048
NBLK = 16
SUMS = 128


def paired_fields(base_key):
    mixed_key = jax.random.fold_in(base_key, 11)
    first_key, second_key = jax.random.split(mixed_key, 2)
    field_shape = (SAMPLES, TOKENS, HEADS * HSIZE)
    query_draw = jnp.clip(jax.random.normal(first_key, field_shape, jnp.float32), -6.0, 6.0)
    key_draw = jnp.clip(jax.random.normal(second_key, field_shape, jnp.float32), -6.0, 6.0)
    return (query_draw, key_draw)


def draw_query_rows(key, part):
    return paired_fields(key)[0].astype(jnp.bfloat16)


def draw_key_rows(key, part):
    return paired_fields(key)[1].astype(jnp.bfloat16)


def draw_pattern(key, part):
    keeping = jax.random.randint(jax.random.fold_in(key, 37), (SAMPLES, NBLK, 3), 0, 5) < 3
    slot_ids = jnp.arange(3, dtype=jnp.int32)[None, None, :]
    blocks = jnp.arange(NBLK, dtype=jnp.int32)[None, :, None] + slot_ids - 1
    inside = (blocks >= 0) & (blocks < NBLK)
    keeping = keeping | (slot_ids == 1)
    return jnp.where(keeping & inside, blocks, -1).astype(jnp.int32)


def draw_block_view(key, part):
    first_key, second_key = jax.random.split(jax.random.fold_in(key, 23))
    start_view = jax.random.randint(first_key, (SAMPLES, 1), 0, NVIEW)
    advances = jax.random.randint(second_key, (SAMPLES, NBLK), 0, 2)
    start_view = start_view.at[0, 0].set(NVIEW - 1)
    advances = advances.at[0, 0].set(0).at[0, 1].set(1)
    return ((start_view + jnp.cumsum(advances, axis=1)) % NVIEW).astype(jnp.int32)


def set_ends(result, own_key, smallest, top_value):
    spot = [jax.random.randint(jax.random.fold_in(own_key, axis), (), 0, length) for axis, length in enumerate(result.shape)]
    widest = result.shape.index(max(result.shape))
    next_to = spot[:widest] + [(spot[widest] + 1) % result.shape[widest]] + spot[widest + 1:]
    return result.at[tuple(spot)].set(smallest).at[tuple(next_to)].set(top_value)


def shard_levels(stream_key, dims, pieces, smallest, high):
    gain, own = 1.0, jax.random.fold_in(stream_key, 6)
    for axis_at, blocks in pieces:
        steps = jnp.exp(jax.random.uniform(jax.random.fold_in(own, axis_at), (blocks,), jnp.float32, smallest / len(pieces), high / len(pieces)))
        gain = gain * jnp.repeat(steps, dims[axis_at] // blocks).reshape([-1 if axis == axis_at else 1 for axis in range(len(dims))])
    return gain


def centred(stream_key, shape, scale, most, cuts=(), held_as=jnp.bfloat16):
    entries = jax.random.normal(stream_key, shape, jnp.float32) * scale
    if len(cuts) > 0:
        entries = shard_levels(stream_key, shape, cuts, -0.22, 0.18) * entries
    return jnp.clip(entries, min=-most, max=most).astype(held_as)


def setup_inputs(seed: int = 0) -> dict:
    arg_keys = jax.random.split(jax.random.key(seed), 11)
    query_rows = draw_query_rows(jax.random.fold_in(arg_keys[10], 71), 0)
    key_rows = draw_key_rows(jax.random.fold_in(arg_keys[10], 71), 0)
    value_rows = centred(arg_keys[2], (SAMPLES, TOKENS, HEADS * HSIZE), 1.0, 6.0, ((0, 16), (1, 16), (2, 2)))
    summary_keys = centred(arg_keys[3], (SAMPLES, SUMS, HEADS * HSIZE), 1.0, 6.0, ((0, 16), (1, 16), (2, 2)))
    summary_values = centred(arg_keys[4], (SAMPLES, SUMS, HEADS * HSIZE), 1.0, 6.0, ((0, 16), (1, 16), (2, 2)))
    out_grad = centred(arg_keys[5], (SAMPLES, TOKENS, HEADS * HSIZE), 1.0, 6.0, ((0, 16), (1, 16), (2, 2)))
    rel_bias = jnp.clip(jax.random.uniform(arg_keys[6], (NREL, HEADS), jnp.float32, -2.0, 2.0) * shard_levels(arg_keys[6], (NREL, HEADS), ((1, 16),), -0.4, 0.0), -2.0, 2.0)
    pattern = draw_pattern(jax.random.fold_in(arg_keys[10], 71), 0)
    block_view = draw_block_view(jax.random.fold_in(arg_keys[10], 71), 0)
    summary_view = set_ends(jax.random.randint(arg_keys[9], (SAMPLES, SUMS), 0, NVIEW), jax.random.fold_in(arg_keys[9], 1), 0, NVIEW - 1).astype(jnp.int32)
    return dict(query_rows=query_rows, key_rows=key_rows, value_rows=value_rows, summary_keys=summary_keys, summary_values=summary_values, out_grad=out_grad, rel_bias=rel_bias, pattern=pattern, block_view=block_view, summary_view=summary_view)


NEG_FILL = -1e+30
HIGH = lax.Precision.HIGHEST

def cycle_class(view_a, view_b):
    distance = jnp.abs(view_a - view_b)
    distance = jnp.minimum(distance, NVIEW - distance)
    return (distance >= 1).astype(jnp.int32) + (distance >= 2).astype(jnp.int32) + (distance >= 8).astype(jnp.int32)

def weighted_sum(weights, win_side, sum_side, split_at):
    first_part = jnp.einsum('nhqk,nkhd->nqhd', weights[..., :split_at].astype(jnp.float32), win_side.astype(jnp.float32), precision=HIGH)
    second_part = jnp.einsum('nhqk,khd->nqhd', weights[..., split_at:].astype(jnp.float32), sum_side.astype(jnp.float32), precision=HIGH)
    return first_part + second_part

def pair_products(left_rows, win_side, sum_side):
    first_part = jnp.einsum('nqhd,nkhd->nhqk', left_rows.astype(jnp.float32), win_side.astype(jnp.float32), precision=HIGH)
    second_part = jnp.einsum('nqhd,khd->nhqk', left_rows.astype(jnp.float32), sum_side.astype(jnp.float32), precision=HIGH)
    return jnp.concatenate([first_part, second_part], axis=3)

def one_sample(sample_items, bias_table):
    query_rows, key_rows, value_rows, summary_keys, summary_values, out_grad, pattern, block_view, summary_view = sample_items
    block_shape = (NBLK, BLK, HEADS, HSIZE)
    split_at = 3 * BLK
    score_scale = 1.0 / math.sqrt(HSIZE)
    queries = query_rows.reshape(block_shape)
    grads_out = out_grad.reshape(block_shape)
    zero_block = jnp.zeros((1, BLK, HEADS, HSIZE), key_rows.dtype)

    def windows(blocks):
        padded = jnp.concatenate([zero_block, blocks, zero_block], axis=0)
        return jnp.concatenate([padded[:-2], padded[1:-1], padded[2:]], axis=1)
    keys_win = windows(key_rows.reshape(block_shape))
    values_win = windows(value_rows.reshape(block_shape))
    keys_sum = summary_keys.reshape(SUMS, HEADS, HSIZE)
    values_sum = summary_values.reshape(SUMS, HEADS, HSIZE)
    padded_views = jnp.pad(block_view, 1)
    near_views = jnp.stack([padded_views[:-2], padded_views[1:-1], padded_views[2:]], axis=1)
    classes = jnp.concatenate([jnp.repeat(cycle_class(block_view[:, None], near_views), BLK, axis=1), cycle_class(block_view[:, None], summary_view[None, :])], axis=1)
    onehot = (classes[:, :, None] == jnp.arange(NREL, dtype=jnp.int32)[None, None, :]).astype(jnp.float32)
    bias = jnp.einsum('nkc,ch->nhk', onehot, bias_table, precision=HIGH)[:, :, None, :]
    allowed = jnp.concatenate([jnp.repeat(pattern >= 0, BLK, axis=1), jnp.ones((NBLK, SUMS), dtype=bool)], axis=1)
    scores = pair_products(queries, keys_win, keys_sum) * score_scale + bias
    scores = jnp.where(allowed[:, None, None, :], scores, NEG_FILL)
    row_max = lax.optimization_barrier(jnp.max(scores, axis=3, keepdims=True))
    lifted = jnp.exp(scores - row_max)
    row_total = lax.optimization_barrier(jnp.sum(lifted, axis=3, keepdims=True))
    weights = lifted / row_total
    weights_low = weights.astype(jnp.bfloat16)
    attended = weighted_sum(weights_low, values_win, values_sum, split_at).astype(jnp.bfloat16)
    prob_grad = pair_products(grads_out, values_win, values_sum)
    row_delta = lax.optimization_barrier(jnp.sum(weights * prob_grad, axis=3, keepdims=True))
    score_grad = weights * (prob_grad - row_delta)
    grad_low = score_grad.astype(jnp.bfloat16)
    query_grad = (weighted_sum(grad_low, keys_win, keys_sum, split_at) * score_scale).astype(jnp.bfloat16)
    win_key = jnp.einsum('nhqk,nqhd->nkhd', grad_low[..., :split_at].astype(jnp.float32), queries.astype(jnp.float32), precision=HIGH)
    win_value = jnp.einsum('nhqk,nqhd->nkhd', weights_low[..., :split_at].astype(jnp.float32), grads_out.astype(jnp.float32), precision=HIGH)
    zero_wide = jnp.zeros((1, BLK, HEADS, HSIZE), jnp.float32)

    def fold_window(window_grad):
        slots = window_grad.reshape(NBLK, 3, BLK, HEADS, HSIZE)
        return slots[:, 1] + jnp.concatenate([slots[1:, 0], zero_wide], axis=0) + jnp.concatenate([zero_wide, slots[:-1, 2]], axis=0)
    key_grad = (fold_window(win_key) * score_scale).astype(jnp.bfloat16)
    value_grad = fold_window(win_value).astype(jnp.bfloat16)
    summary_key_grad = (jnp.einsum('nhqk,nqhd->khd', grad_low[..., split_at:].astype(jnp.float32), queries.astype(jnp.float32), precision=HIGH) * score_scale).astype(jnp.bfloat16)
    summary_value_grad = jnp.einsum('nhqk,nqhd->khd', weights_low[..., split_at:].astype(jnp.float32), grads_out.astype(jnp.float32), precision=HIGH).astype(jnp.bfloat16)
    bias_term = jnp.einsum('nhqk,nkc->ch', score_grad, onehot, precision=HIGH)
    width = HEADS * HSIZE
    return (attended.reshape(TOKENS, width), query_grad.reshape(TOKENS, width), key_grad.reshape(TOKENS, width), value_grad.reshape(TOKENS, width), summary_key_grad.reshape(SUMS, width), summary_value_grad.reshape(SUMS, width), bias_term)

def reference(query_rows, key_rows, value_rows, summary_keys, summary_values, out_grad, rel_bias, pattern, block_view, summary_view):
    results = lax.map(functools.partial(one_sample, bias_table=rel_bias), (query_rows, key_rows, value_rows, summary_keys, summary_values, out_grad, pattern, block_view, summary_view))
    return (results[0], results[1], results[2], results[3], results[4], results[5], lax.optimization_barrier(jnp.sum(results[6], axis=0)))
```

```python
import functools
import math

import jax
import jax.numpy as jnp
from jax import lax
from jax.experimental import pallas as pl
from jax.experimental.pallas import tpu as pltpu
from jax.sharding import PartitionSpec as P

HSIZE = 128
BLK = 128
NVIEW = 96
NREL = 4
NEG_FILL = -1e30
SCALE = 1.0 / math.sqrt(HSIZE)


def view_class(view_a, view_b):
    distance = jnp.abs(view_a - view_b)
    distance = jnp.minimum(distance, NVIEW - distance)
    one = jnp.int32(1)
    zero = jnp.int32(0)
    return (
        jnp.where(distance >= 1, one, zero)
        + jnp.where(distance >= 2, one, zero)
        + jnp.where(distance >= 8, one, zero)
    )


def dot_nt(left, right):
    return lax.dot_general(left, right, (((1,), (1,)), ((), ())), preferred_element_type=jnp.float32)


def dot_nn(left, right):
    return lax.dot_general(left, right, (((1,), (0,)), ((), ())), preferred_element_type=jnp.float32)


def dot_tn(left, right):
    return lax.dot_general(left, right, (((0,), (0,)), ((), ())), preferred_element_type=jnp.float32)


def attention_kernel(
    heads,
    nblk,
    place,
    pattern,
    views,
    table,
    sum_views,
    query,
    grad_out,
    own_kv,
    left_kv,
    right_kv,
    sums,
    attended,
    query_grad,
    to_left,
    to_right,
    own_grad,
    sum_grad,
    bias_part,
):
    block = place[0]
    head_start = place[1]
    own_view = views[block]
    slot_views = [
        views[jnp.maximum(block - 1, 0)],
        own_view,
        views[jnp.minimum(block + 1, nblk - 1)],
    ]
    slot_class = [view_class(own_view, view) for view in slot_views]
    slot_mask = [
        jnp.where(pattern[block, slot] >= 0, jnp.float32(0.0), jnp.float32(NEG_FILL))
        for slot in range(3)
    ]
    sum_class = view_class(own_view, sum_views[...])
    count, rows = sums.shape[0], sums.shape[1] // 2
    bias_part[...] = jnp.zeros_like(bias_part)
    class_row = lax.broadcasted_iota(jnp.int32, (8, BLK), 0)
    for head in range(heads):
        cols = slice(head * HSIZE, (head + 1) * HSIZE)
        q = query[:, cols]
        go = grad_out[:, cols]
        keys = jnp.concatenate(
            [
                left_kv[0, :, cols],
                own_kv[0, :, cols],
                right_kv[0, :, cols],
                sums[:, :rows, cols].reshape(count * rows, HSIZE),
            ],
            axis=0,
        )
        values = jnp.concatenate(
            [
                left_kv[1, :, cols],
                own_kv[1, :, cols],
                right_kv[1, :, cols],
                sums[:, rows:, cols].reshape(count * rows, HSIZE),
            ],
            axis=0,
        )
        biases = [table[head_start + head, c] for c in range(NREL)]

        def pick(cls):
            low = jnp.where(cls == 0, biases[0], biases[1])
            high = jnp.where(cls == 2, biases[2], biases[3])
            return jnp.where(cls < 2, low, high)

        raw = dot_nt(keys, q) * SCALE
        scores = jnp.concatenate(
            [
                raw[slot * BLK : (slot + 1) * BLK] + (pick(slot_class[slot]) + slot_mask[slot])
                for slot in range(3)
            ]
            + [raw[3 * BLK :] + pick(sum_class)],
            axis=0,
        )
        row_max = jnp.max(scores, axis=0, keepdims=True)
        lifted = jnp.exp(scores - row_max)
        weights = lifted * (1.0 / jnp.sum(lifted, axis=0, keepdims=True))
        low = weights.astype(jnp.bfloat16)
        prob_grad = dot_nt(values, go)
        row_delta = jnp.sum(weights * prob_grad, axis=0, keepdims=True)
        score_grad = weights * (prob_grad - row_delta)
        grad_low = score_grad.astype(jnp.bfloat16)
        attended[:, cols] = dot_tn(low, values).astype(jnp.bfloat16)
        query_grad[:, cols] = (dot_tn(grad_low, keys) * SCALE).astype(jnp.bfloat16)
        key_terms = dot_nn(grad_low, q)
        value_terms = dot_nn(low, go)
        for index, terms in enumerate((key_terms, value_terms)):
            to_left[index, :, cols] = terms[:BLK].astype(jnp.bfloat16)
            own_grad[index, :, cols] = terms[BLK : 2 * BLK]
            to_right[index, :, cols] = terms[2 * BLK : 3 * BLK].astype(jnp.bfloat16)
            sum_grad[:, index * rows : (index + 1) * rows, cols] = (
                terms[3 * BLK :].astype(jnp.bfloat16).reshape(count, rows, HSIZE)
            )
        slot_sums = [
            jnp.sum(score_grad[slot * BLK : (slot + 1) * BLK], axis=0, keepdims=True)
            for slot in range(3)
        ]
        sum_part = score_grad[3 * BLK :]
        tile = jnp.zeros((8, BLK), jnp.float32)
        for c in range(NREL):
            line = jnp.sum(jnp.where(sum_class == c, sum_part, 0.0), axis=0, keepdims=True)
            for slot in range(3):
                line = line + jnp.where(slot_class[slot] == c, slot_sums[slot], 0.0)
            tile = jnp.where(class_row == c, line, tile)
        total = jnp.broadcast_to(jnp.sum(tile, axis=1, keepdims=True), (8, BLK))
        for copy in range(2):
            bias_part[2 * (head_start + head) + copy] = total


def body(
    query_rows,
    key_rows,
    value_rows,
    summary_keys,
    summary_values,
    out_grad,
    rel_bias,
    pattern,
    block_view,
    summary_view,
):
    tok_rows, width = query_rows.shape[1:]
    heads = width // HSIZE
    nseq = lax.axis_size("seq")
    nfsdp = lax.axis_size("fsdp")
    ndp = lax.axis_size("dp")
    nblk = block_view.shape[1]
    sum_rows = summary_keys.shape[1]
    bf16, f32 = jnp.bfloat16, jnp.float32

    up = [(i, i + 1) for i in range(nseq - 1)]
    down = [(i + 1, i) for i in range(nseq - 1)]
    own_kv = jnp.stack([key_rows[0], value_rows[0]])
    left_kv = lax.ppermute(own_kv, "seq", up)
    right_kv = lax.ppermute(own_kv, "seq", down)
    own_sums = jnp.concatenate([summary_keys[0], summary_values[0]], axis=0)
    sums = lax.all_to_all(
        jnp.broadcast_to(own_sums[None], (nseq, 2 * sum_rows, width)), "seq", 0, 0, tiled=True
    )
    table = lax.all_to_all(
        jnp.broadcast_to(rel_bias.reshape(1, NREL), (nfsdp, NREL)), "fsdp", 0, 0, tiled=True
    )
    place = jnp.stack([lax.axis_index("seq"), lax.axis_index("dp") * heads]).astype(jnp.int32)

    smem = pl.BlockSpec(memory_space=pltpu.SMEM)
    vmem = pl.BlockSpec(memory_space=pltpu.VMEM)
    shaped = jax.ShapeDtypeStruct
    attended, query_grad, to_left, to_right, own_grad, sum_grad, bias_part = pl.pallas_call(
        functools.partial(attention_kernel, heads, nblk),
        out_shape=(
            shaped((tok_rows, width), bf16),
            shaped((tok_rows, width), bf16),
            shaped((2, BLK, width), bf16),
            shaped((2, BLK, width), bf16),
            shaped((2, BLK, width), f32),
            shaped((nseq, 2 * sum_rows, width), bf16),
            shaped((nfsdp * ndp, 8, BLK), f32),
        ),
        in_specs=[smem] * 4 + [vmem] * 7,
        out_specs=(vmem,) * 7,
        name="attention",
    )(
        place,
        pattern[0],
        block_view[0],
        table,
        summary_view.reshape(-1, 1),
        query_rows[0],
        out_grad[0],
        own_kv,
        left_kv,
        right_kv,
        sums,
    )
    from_right = lax.ppermute(to_left, "seq", down)
    from_left = lax.ppermute(to_right, "seq", up)
    sum_terms = lax.all_to_all(sum_grad, "seq", 0, 0, tiled=True)
    bias_part = lax.all_to_all(bias_part, ("fsdp", "dp"), 0, 0, tiled=True)
    bias_mine = jnp.sum(bias_part, axis=0, keepdims=True)
    bias_all = lax.all_to_all(
        jnp.broadcast_to(bias_mine, (nseq, 8, BLK)), "seq", 0, 0, tiled=True
    )
    bias_grad = jnp.sum(bias_all, axis=0)[:NREL, :1]

    grads = own_grad + from_left.astype(f32) + from_right.astype(f32)
    key_grad = (grads[0] * SCALE).astype(bf16)
    value_grad = grads[1].astype(bf16)
    summary = jnp.sum(sum_terms.astype(f32), axis=0)
    summary_key_grad = (summary[:sum_rows] * SCALE).astype(bf16)
    summary_value_grad = summary[sum_rows:].astype(bf16)
    return (
        attended[None],
        query_grad[None],
        key_grad[None],
        value_grad[None],
        summary_key_grad[None],
        summary_value_grad[None],
        bias_grad,
    )


def solution(mesh):
    rows = P("fsdp", "seq", "dp")
    return jax.shard_map(
        body,
        mesh=mesh,
        in_specs=(rows,) * 6
        + (P(None, "fsdp"), P("fsdp", None, None), P("fsdp", None), P("fsdp", None)),
        out_specs=(rows,) * 6 + (P(None, "fsdp"),),
        check_vma=False,
    )
```

```python
import functools
import math

import jax
import jax.numpy as jnp
from jax import lax
from jax.experimental import pallas as pl
from jax.experimental.pallas import tpu as pltpu
from jax.sharding import PartitionSpec as P


HSIZE = 128
BLK = 128
NVIEW = 96
NREL = 4
NEG_FILL = -1e30
SCALE = 1.0 / math.sqrt(HSIZE)


def view_class(view_a, view_b):
    distance = jnp.abs(view_a - view_b)
    distance = jnp.minimum(distance, NVIEW - distance)
    one = jnp.int32(1)
    zero = jnp.int32(0)
    return (
        jnp.where(distance >= 1, one, zero)
        + jnp.where(distance >= 2, one, zero)
        + jnp.where(distance >= 8, one, zero)
    )


def dot_nt(left, right):
    return lax.dot_general(left, right, (((1,), (1,)), ((), ())), preferred_element_type=jnp.float32)


def dot_nn(left, right):
    return lax.dot_general(left, right, (((1,), (0,)), ((), ())), preferred_element_type=jnp.float32)


def dot_tn(left, right):
    return lax.dot_general(left, right, (((0,), (0,)), ((), ())), preferred_element_type=jnp.float32)


def attention_kernel(
    heads,
    nblk,
    ndp,
    place,
    pattern,
    views,
    table,
    sum_views,
    query,
    grad_out,
    own_kv,
    left_kv,
    right_kv,
    sums,
    attended,
    query_grad,
    to_left,
    to_right,
    own_grad,
    sum_grad,
    bias_part,
):
    block = place[0]
    head_start = place[1]
    own_view = views[block]
    slot_views = [
        views[jnp.maximum(block - 1, 0)],
        own_view,
        views[jnp.minimum(block + 1, nblk - 1)],
    ]
    slot_class = [view_class(own_view, view) for view in slot_views]
    slot_mask = [
        jnp.where(pattern[block, slot] >= 0, jnp.float32(0.0), jnp.float32(NEG_FILL))
        for slot in range(3)
    ]
    sum_class = view_class(own_view, sum_views[...])
    count, rows = sums.shape[0], sums.shape[1] // 2
    bias_part[...] = jnp.zeros_like(bias_part)
    ride = heads * HSIZE
    sum_grad[:, :, ride:] = jnp.zeros((count, 2 * rows, BLK), jnp.bfloat16)
    class_row = lax.broadcasted_iota(jnp.int32, (8, BLK), 0)
    class_lane = lax.broadcasted_iota(jnp.int32, (8, BLK), 1)
    for head in range(heads):
        cols = slice(head * HSIZE, (head + 1) * HSIZE)
        q = query[:, cols]
        go = grad_out[:, cols]
        keys = jnp.concatenate(
            [
                left_kv[0, :, cols],
                own_kv[0, :, cols],
                right_kv[0, :, cols],
                sums[:, :rows, cols].reshape(count * rows, HSIZE),
            ],
            axis=0,
        )
        values = jnp.concatenate(
            [
                left_kv[1, :, cols],
                own_kv[1, :, cols],
                right_kv[1, :, cols],
                sums[:, rows:, cols].reshape(count * rows, HSIZE),
            ],
            axis=0,
        )
        biases = [table[c, head_start + head] for c in range(NREL)]

        def pick(cls):
            low = jnp.where(cls == 0, biases[0], biases[1])
            high = jnp.where(cls == 2, biases[2], biases[3])
            return jnp.where(cls < 2, low, high)

        raw = dot_nt(keys, q) * SCALE
        scores = jnp.concatenate(
            [
                raw[slot * BLK : (slot + 1) * BLK] + (pick(slot_class[slot]) + slot_mask[slot])
                for slot in range(3)
            ]
            + [raw[3 * BLK :] + pick(sum_class)],
            axis=0,
        )
        row_max = jnp.max(scores, axis=0, keepdims=True)
        lifted = jnp.exp(scores - row_max)
        weights = lifted * (1.0 / jnp.sum(lifted, axis=0, keepdims=True))
        low = weights.astype(jnp.bfloat16)
        prob_grad = dot_nt(values, go)
        row_delta = jnp.sum(weights * prob_grad, axis=0, keepdims=True)
        score_grad = weights * (prob_grad - row_delta)
        grad_low = score_grad.astype(jnp.bfloat16)
        attended[:, cols] = dot_tn(low, values).astype(jnp.bfloat16)
        query_grad[:, cols] = (dot_tn(grad_low, keys) * SCALE).astype(jnp.bfloat16)
        key_terms = dot_nn(grad_low, q)
        value_terms = dot_nn(low, go)
        for index, terms in enumerate((key_terms, value_terms)):
            to_left[index, :, cols] = terms[:BLK].astype(jnp.bfloat16)
            own_grad[index, :, cols] = terms[BLK : 2 * BLK]
            to_right[index, :, cols] = terms[2 * BLK : 3 * BLK].astype(jnp.bfloat16)
            sum_grad[:, index * rows : (index + 1) * rows, cols] = (
                terms[3 * BLK :].astype(jnp.bfloat16).reshape(count, rows, HSIZE)
            )
        slot_sums = [
            jnp.sum(score_grad[slot * BLK : (slot + 1) * BLK], axis=0, keepdims=True)
            for slot in range(3)
        ]
        sum_part = score_grad[3 * BLK :]
        tile = jnp.zeros((8, BLK), jnp.float32)
        for c in range(NREL):
            line = jnp.sum(jnp.where(sum_class == c, sum_part, 0.0), axis=0, keepdims=True)
            for slot in range(3):
                line = line + jnp.where(slot_class[slot] == c, slot_sums[slot], 0.0)
            tile = jnp.where(class_row == c, line, tile)
        totals = jnp.where(class_row == class_lane, jnp.sum(tile, axis=1, keepdims=True), 0.0)
        line = jnp.sum(totals, axis=0, keepdims=True)
        for copy in range(ndp):
            bias_part[ndp * (head_start + head) + copy] = line


def body(
    query_rows,
    key_rows,
    value_rows,
    summary_keys,
    summary_values,
    out_grad,
    rel_bias,
    pattern,
    block_view,
    summary_view,
):
    tok_rows, width = query_rows.shape[1:]
    heads = width // HSIZE
    nseq = lax.axis_size("seq")
    nfsdp = lax.axis_size("fsdp")
    ndp = lax.axis_size("dp")
    nblk = block_view.shape[1]
    sum_rows = summary_keys.shape[1]
    bf16, f32 = jnp.bfloat16, jnp.float32

    up = [(i, i + 1) for i in range(nseq - 1)]
    down = [(i + 1, i) for i in range(nseq - 1)]
    own_kv = jnp.stack([key_rows[0], value_rows[0]])
    left_kv = lax.ppermute(own_kv, "seq", up)
    right_kv = lax.ppermute(own_kv, "seq", down)
    own_sums = jnp.concatenate([summary_keys[0], summary_values[0]], axis=0)
    sums_out = jnp.broadcast_to(own_sums[None], (nseq, 2 * sum_rows, width))
    sums = lax.all_to_all(sums_out, "seq", 0, 0, tiled=True)
    table = lax.all_gather(rel_bias, "fsdp", axis=1, tiled=True)
    place = jnp.stack([lax.axis_index("seq"), lax.axis_index("dp") * heads]).astype(jnp.int32)

    smem = pl.BlockSpec(memory_space=pltpu.SMEM)
    vmem = pl.BlockSpec(memory_space=pltpu.VMEM)
    shaped = jax.ShapeDtypeStruct
    attended, query_grad, to_left, to_right, own_grad, sum_grad, bias_part = pl.pallas_call(
        functools.partial(attention_kernel, heads, nblk, ndp),
        out_shape=(
            shaped((tok_rows, width), bf16),
            shaped((tok_rows, width), bf16),
            shaped((2, BLK, width), bf16),
            shaped((2, BLK, width), bf16),
            shaped((2, BLK, width), f32),
            shaped((nseq, 2 * sum_rows, width + BLK), bf16),
            shaped((nfsdp * ndp, 1, BLK), f32),
        ),
        in_specs=[smem] * 4 + [vmem] * 7,
        out_specs=(vmem,) * 7,
        name="attention",
    )(
        place,
        pattern[0],
        block_view[0],
        table,
        summary_view.reshape(-1, 1),
        query_rows[0],
        out_grad[0],
        own_kv,
        left_kv,
        right_kv,
        sums,
    )
    from_right = lax.ppermute(to_left, "seq", down)
    from_left = lax.ppermute(to_right, "seq", up)
    bias_part = lax.all_to_all(bias_part, ("fsdp", "dp"), 0, 0, tiled=True)
    rest = jnp.sum(bias_part, axis=0)
    pieces = []
    for _ in range(3):
        pieces.append(lax.reduce_precision(rest, 8, 7))
        rest = rest - pieces[-1]
    rider = jnp.pad(jnp.concatenate(pieces, axis=0).astype(bf16), ((0, 2 * sum_rows - 3), (0, 0)))
    rider = jnp.broadcast_to(rider[None], (nseq, 2 * sum_rows, BLK))
    sum_grad = lax.dynamic_update_slice(sum_grad, rider, (0, 0, width))
    sum_terms = lax.all_to_all(sum_grad, "seq", 0, 0, tiled=True)

    grads = own_grad + from_left.astype(f32) + from_right.astype(f32)
    key_grad = (grads[0] * SCALE).astype(bf16)
    value_grad = grads[1].astype(bf16)
    summary = jnp.sum(sum_terms.astype(f32), axis=0)
    summary_key_grad = (summary[:sum_rows, :width] * SCALE).astype(bf16)
    summary_value_grad = summary[sum_rows:, :width].astype(bf16)
    bias_grad = jnp.sum(summary[:3, width : width + NREL], axis=0).reshape(NREL, 1)
    return (
        attended[None],
        query_grad[None],
        key_grad[None],
        value_grad[None],
        summary_key_grad[None],
        summary_value_grad[None],
        bias_grad,
    )


def solution(mesh):
    rows = P("fsdp", "seq", "dp")
    return jax.shard_map(
        body,
        mesh=mesh,
        in_specs=(rows,) * 6
        + (P(None, "fsdp"), P("fsdp", None, None), P("fsdp", None), P("fsdp", None)),
        out_specs=(rows,) * 6 + (P(None, "fsdp"),),
        check_vma=False,
    )
```

```python
import functools
import math

import jax
import jax.numpy as jnp
from jax import lax
from jax.experimental import pallas as pl
from jax.experimental.pallas import tpu as pltpu
from jax.sharding import PartitionSpec as P


HSIZE = 128
BLK = 128
NVIEW = 96
NREL = 4
RIDE = 8
NEG_FILL = -1e30
SCALE = 1.0 / math.sqrt(HSIZE)


def view_class(view_a, view_b):
    distance = jnp.abs(view_a - view_b)
    distance = jnp.minimum(distance, NVIEW - distance)
    one = jnp.int32(1)
    zero = jnp.int32(0)
    return (
        jnp.where(distance >= 1, one, zero)
        + jnp.where(distance >= 2, one, zero)
        + jnp.where(distance >= 8, one, zero)
    )


def dot_nt(left, right):
    return lax.dot_general(left, right, (((1,), (1,)), ((), ())), preferred_element_type=jnp.float32)


def dot_nn(left, right):
    return lax.dot_general(left, right, (((1,), (0,)), ((), ())), preferred_element_type=jnp.float32)


def dot_tn(left, right):
    return lax.dot_general(left, right, (((0,), (0,)), ((), ())), preferred_element_type=jnp.float32)


def attention_kernel(
    heads,
    nblk,
    ndp,
    place,
    pattern,
    views,
    table,
    sum_views,
    query,
    grad_out,
    own_kv,
    left_kv,
    right_kv,
    sums,
    attended,
    query_grad,
    to_left,
    to_right,
    own_grad,
    sum_grad,
    bias_part,
):
    block = place[0]
    head_start = place[1]
    own_view = views[block]
    slot_views = [
        views[jnp.maximum(block - 1, 0)],
        own_view,
        views[jnp.minimum(block + 1, nblk - 1)],
    ]
    slot_class = [view_class(own_view, view) for view in slot_views]
    slot_mask = [
        jnp.where(pattern[block, slot] >= 0, jnp.float32(0.0), jnp.float32(NEG_FILL))
        for slot in range(3)
    ]
    sum_class = view_class(own_view, sum_views[...])
    count, rows = sums.shape[0], sums.shape[1] // 2
    bias_part[...] = jnp.zeros_like(bias_part)
    class_row = lax.broadcasted_iota(jnp.int32, (8, BLK), 0)
    class_lane = lax.broadcasted_iota(jnp.int32, (8, BLK), 1)
    for head in range(heads):
        cols = slice(head * HSIZE, (head + 1) * HSIZE)
        late = slice((heads + head) * HSIZE, (heads + head + 1) * HSIZE)
        q = query[:, cols]
        go = grad_out[:, cols]
        keys = jnp.concatenate(
            [
                left_kv[:, cols],
                own_kv[:, cols],
                right_kv[:, cols],
                sums[:, :rows, cols].reshape(count * rows, HSIZE),
            ],
            axis=0,
        )
        values = jnp.concatenate(
            [
                left_kv[:, late],
                own_kv[:, late],
                right_kv[:, late],
                sums[:, rows:, cols].reshape(count * rows, HSIZE),
            ],
            axis=0,
        )
        biases = [table[head_start + head, c] for c in range(NREL)]

        def pick(cls):
            low = jnp.where(cls == 0, biases[0], biases[1])
            high = jnp.where(cls == 2, biases[2], biases[3])
            return jnp.where(cls < 2, low, high)

        raw = dot_nt(keys, q) * SCALE
        scores = jnp.concatenate(
            [
                raw[slot * BLK : (slot + 1) * BLK] + (pick(slot_class[slot]) + slot_mask[slot])
                for slot in range(3)
            ]
            + [raw[3 * BLK :] + pick(sum_class)],
            axis=0,
        )
        row_max = jnp.max(scores, axis=0, keepdims=True)
        lifted = jnp.exp(scores - row_max)
        weights = lifted * (1.0 / jnp.sum(lifted, axis=0, keepdims=True))
        low = weights.astype(jnp.bfloat16)
        prob_grad = dot_nt(values, go)
        row_delta = jnp.sum(weights * prob_grad, axis=0, keepdims=True)
        score_grad = weights * (prob_grad - row_delta)
        grad_low = score_grad.astype(jnp.bfloat16)
        attended[:, cols] = dot_tn(low, values).astype(jnp.bfloat16)
        query_grad[:, cols] = (dot_tn(grad_low, keys) * SCALE).astype(jnp.bfloat16)
        key_terms = dot_nn(grad_low, q)
        value_terms = dot_nn(low, go)
        for index, (terms, where) in enumerate(((key_terms, cols), (value_terms, late))):
            to_left[:, where] = terms[:BLK].astype(jnp.bfloat16)
            own_grad[:, where] = terms[BLK : 2 * BLK]
            to_right[:, where] = terms[2 * BLK : 3 * BLK].astype(jnp.bfloat16)
            first = (index * heads + head) * rows
            sum_grad[:, first : first + rows] = (
                terms[3 * BLK :].astype(jnp.bfloat16).reshape(count, rows, HSIZE)
            )
        slot_sums = [
            jnp.sum(score_grad[slot * BLK : (slot + 1) * BLK], axis=0, keepdims=True)
            for slot in range(3)
        ]
        sum_part = score_grad[3 * BLK :]
        tile = jnp.zeros((8, BLK), jnp.float32)
        for c in range(NREL):
            line = jnp.sum(jnp.where(sum_class == c, sum_part, 0.0), axis=0, keepdims=True)
            for slot in range(3):
                line = line + jnp.where(slot_class[slot] == c, slot_sums[slot], 0.0)
            tile = jnp.where(class_row == c, line, tile)
        totals = jnp.where(class_row == class_lane, jnp.sum(tile, axis=1, keepdims=True), 0.0)
        line = jnp.sum(totals, axis=0, keepdims=True)
        for copy in range(ndp):
            bias_part[ndp * (head_start + head) + copy] = line


def finish_kernel(heads, rows, terms, key_grad, value_grad, bias_grad):
    def total(first, size):
        parts = [terms[i, first : first + size].astype(jnp.float32) for i in range(terms.shape[0])]
        while len(parts) > 1:
            parts = [parts[i] + parts[i + 1] for i in range(0, len(parts), 2)]
        return parts[0]

    for head in range(heads):
        cols = slice(head * HSIZE, (head + 1) * HSIZE)
        key_grad[:, cols] = (total(head * rows, rows) * SCALE).astype(jnp.bfloat16)
        value_grad[:, cols] = total((heads + head) * rows, rows).astype(jnp.bfloat16)
    pieces = jnp.sum(total(2 * heads * rows, RIDE), axis=0, keepdims=True)
    bias_grad[...] = pieces[:, :NREL]


def body(
    query_rows,
    key_rows,
    value_rows,
    summary_keys,
    summary_values,
    out_grad,
    rel_bias,
    pattern,
    block_view,
    summary_view,
):
    tok_rows, width = query_rows.shape[1:]
    heads = width // HSIZE
    nseq = lax.axis_size("seq")
    nfsdp = lax.axis_size("fsdp")
    ndp = lax.axis_size("dp")
    nblk = block_view.shape[1]
    sum_rows = summary_keys.shape[1]
    bf16, f32 = jnp.bfloat16, jnp.float32

    up = [(i, i + 1) for i in range(nseq - 1)]
    down = [(i + 1, i) for i in range(nseq - 1)]
    table_out = jnp.broadcast_to(rel_bias.reshape(1, NREL), (nfsdp, NREL))
    table = lax.all_to_all(table_out, "fsdp", 0, 0, tiled=True)
    own_kv = jnp.concatenate([key_rows[0], value_rows[0]], axis=1)
    left_kv = lax.ppermute(own_kv, "seq", up)
    right_kv = lax.ppermute(own_kv, "seq", down)
    own_sums = jnp.concatenate([summary_keys[0], summary_values[0]], axis=0)
    sums_out = jnp.broadcast_to(own_sums[None], (nseq, 2 * sum_rows, width))
    sums = lax.all_to_all(sums_out, "seq", 0, 0, tiled=True)
    place = jnp.stack([lax.axis_index("seq"), lax.axis_index("dp") * heads]).astype(jnp.int32)

    smem = pl.BlockSpec(memory_space=pltpu.SMEM)
    vmem = pl.BlockSpec(memory_space=pltpu.VMEM)
    shaped = jax.ShapeDtypeStruct
    attended, query_grad, to_left, to_right, own_grad, sum_grad, bias_part = pl.pallas_call(
        functools.partial(attention_kernel, heads, nblk, ndp),
        out_shape=(
            shaped((tok_rows, width), bf16),
            shaped((tok_rows, width), bf16),
            shaped((BLK, 2 * width), bf16),
            shaped((BLK, 2 * width), bf16),
            shaped((BLK, 2 * width), f32),
            shaped((nseq, 2 * heads * sum_rows + RIDE, HSIZE), bf16),
            shaped((nfsdp * ndp, 1, BLK), f32),
        ),
        in_specs=[smem] * 4 + [vmem] * 7,
        out_specs=(vmem,) * 7,
        name="attention",
    )(
        place,
        pattern[0],
        block_view[0],
        table,
        summary_view.reshape(-1, 1),
        query_rows[0],
        out_grad[0],
        own_kv,
        left_kv,
        right_kv,
        sums,
    )
    bias_part = lax.all_to_all(bias_part, ("fsdp", "dp"), 0, 0, tiled=True)
    from_right = lax.ppermute(to_left, "seq", down)
    from_left = lax.ppermute(to_right, "seq", up)
    rest = jnp.sum(bias_part, axis=0)
    pieces = []
    for _ in range(3):
        pieces.append(lax.reduce_precision(rest, 8, 7))
        rest = rest - pieces[-1]
    rider = jnp.pad(jnp.concatenate(pieces, axis=0).astype(bf16), ((0, RIDE - 3), (0, 0)))
    rider = jnp.broadcast_to(rider[None], (nseq, RIDE, BLK))
    sum_grad = lax.dynamic_update_slice(sum_grad, rider, (0, 2 * heads * sum_rows, 0))
    sum_terms = lax.all_to_all(sum_grad, "seq", 0, 0, tiled=True)

    grads = own_grad + from_left.astype(f32) + from_right.astype(f32)
    key_grad = (grads[:, :width] * SCALE).astype(bf16)
    value_grad = grads[:, width:].astype(bf16)
    summary_key_grad, summary_value_grad, bias_grad = pl.pallas_call(
        functools.partial(finish_kernel, heads, sum_rows),
        out_shape=(
            shaped((sum_rows, width), bf16),
            shaped((sum_rows, width), bf16),
            shaped((1, NREL), f32),
        ),
        in_specs=[vmem],
        out_specs=(vmem,) * 3,
        name="finish",
    )(sum_terms)
    return (
        attended[None],
        query_grad[None],
        key_grad[None],
        value_grad[None],
        summary_key_grad[None],
        summary_value_grad[None],
        bias_grad.reshape(NREL, 1),
    )


def solution(mesh):
    rows = P("fsdp", "seq", "dp")
    return jax.shard_map(
        body,
        mesh=mesh,
        in_specs=(rows,) * 6
        + (P(None, "fsdp"), P("fsdp", None, None), P("fsdp", None), P("fsdp", None)),
        out_specs=(rows,) * 6 + (P(None, "fsdp"),),
        check_vma=False,
    )
```

```python
import functools
import math

import jax
import jax.numpy as jnp
from jax import lax
from jax.experimental import pallas as pl
from jax.experimental.pallas import tpu as pltpu
from jax.sharding import PartitionSpec as P


HSIZE = 128
BLK = 128
NVIEW = 96
NREL = 4
RIDE = 8
NEG_FILL = -1e30
SCALE = 1.0 / math.sqrt(HSIZE)


def view_class(view_a, view_b):
    distance = jnp.abs(view_a - view_b)
    distance = jnp.minimum(distance, NVIEW - distance)
    one = jnp.int32(1)
    zero = jnp.int32(0)
    return (
        jnp.where(distance >= 1, one, zero)
        + jnp.where(distance >= 2, one, zero)
        + jnp.where(distance >= 8, one, zero)
    )


def dot_nt(left, right):
    return lax.dot_general(left, right, (((1,), (1,)), ((), ())), preferred_element_type=jnp.float32)


def dot_nn(left, right):
    return lax.dot_general(left, right, (((1,), (0,)), ((), ())), preferred_element_type=jnp.float32)


def dot_tn(left, right):
    return lax.dot_general(left, right, (((0,), (0,)), ((), ())), preferred_element_type=jnp.float32)


def attention_kernel(
    heads,
    nblk,
    ndp,
    half,
    place,
    pattern,
    views,
    table,
    sum_views,
    query,
    grad_out,
    own_kv,
    left_kv,
    right_kv,
    cross_key,
    cross_value,
    sums,
    attended,
    query_grad,
    to_left,
    to_right,
    to_cross,
    own_grad,
    sum_grad,
    bias_part,
):
    block = place[0]
    head_start = place[1]
    own_view = views[block]
    slot_views = [
        views[jnp.maximum(block - 1, 0)],
        own_view,
        views[jnp.minimum(block + 1, nblk - 1)],
    ]
    slot_class = [view_class(own_view, view) for view in slot_views]
    slot_mask = [
        jnp.where(pattern[block, slot] >= 0, jnp.float32(0.0), jnp.float32(NEG_FILL))
        for slot in range(3)
    ]
    sum_class = view_class(own_view, sum_views[...])
    count, rows = sums.shape[0], sums.shape[1] // 2
    bias_part[...] = jnp.zeros_like(bias_part)
    class_row = lax.broadcasted_iota(jnp.int32, (8, BLK), 0)
    class_lane = lax.broadcasted_iota(jnp.int32, (8, BLK), 1)
    for head in range(heads):
        cols = slice(head * HSIZE, (head + 1) * HSIZE)
        late = slice((heads + head) * HSIZE, (heads + head + 1) * HSIZE)
        q = query[:, cols]
        go = grad_out[:, cols]
        keys = jnp.concatenate(
            [
                lax.select(block == half, cross_key[:, cols], left_kv[:, cols]),
                own_kv[:, cols],
                lax.select(block == half - 1, cross_key[:, cols], right_kv[:, cols]),
                sums[:, :rows, cols].reshape(count * rows, HSIZE),
            ],
            axis=0,
        )
        values = jnp.concatenate(
            [
                lax.select(block == half, cross_value[:, cols], left_kv[:, late]),
                own_kv[:, late],
                lax.select(block == half - 1, cross_value[:, cols], right_kv[:, late]),
                sums[:, rows:, cols].reshape(count * rows, HSIZE),
            ],
            axis=0,
        )
        biases = [table[head_start + head, c] for c in range(NREL)]

        def pick(cls):
            low = jnp.where(cls == 0, biases[0], biases[1])
            high = jnp.where(cls == 2, biases[2], biases[3])
            return jnp.where(cls < 2, low, high)

        raw = dot_nt(keys, q) * SCALE
        scores = jnp.concatenate(
            [
                raw[slot * BLK : (slot + 1) * BLK] + (pick(slot_class[slot]) + slot_mask[slot])
                for slot in range(3)
            ]
            + [raw[3 * BLK :] + pick(sum_class)],
            axis=0,
        )
        row_max = jnp.max(scores, axis=0, keepdims=True)
        lifted = jnp.exp(scores - row_max)
        weights = lifted * (1.0 / jnp.sum(lifted, axis=0, keepdims=True))
        low = weights.astype(jnp.bfloat16)
        prob_grad = dot_nt(values, go)
        row_delta = jnp.sum(weights * prob_grad, axis=0, keepdims=True)
        score_grad = weights * (prob_grad - row_delta)
        grad_low = score_grad.astype(jnp.bfloat16)
        attended[:, cols] = dot_tn(low, values).astype(jnp.bfloat16)
        query_grad[:, cols] = (dot_tn(grad_low, keys) * SCALE).astype(jnp.bfloat16)
        key_terms = dot_nn(grad_low, q)
        value_terms = dot_nn(low, go)
        for index, (terms, where) in enumerate(((key_terms, cols), (value_terms, late))):
            leftward = terms[:BLK].astype(jnp.bfloat16)
            rightward = terms[2 * BLK : 3 * BLK].astype(jnp.bfloat16)
            to_left[:, where] = leftward
            to_right[:, where] = rightward
            to_cross[index, :, cols] = lax.select(block == half, leftward, rightward)
            own_grad[:, where] = terms[BLK : 2 * BLK]
            first = (index * heads + head) * rows
            sum_grad[:, first : first + rows] = (
                terms[3 * BLK :].astype(jnp.bfloat16).reshape(count, rows, HSIZE)
            )
        slot_sums = [
            jnp.sum(score_grad[slot * BLK : (slot + 1) * BLK], axis=0, keepdims=True)
            for slot in range(3)
        ]
        sum_part = score_grad[3 * BLK :]
        tile = jnp.zeros((8, BLK), jnp.float32)
        for c in range(NREL):
            line = jnp.sum(jnp.where(sum_class == c, sum_part, 0.0), axis=0, keepdims=True)
            for slot in range(3):
                line = line + jnp.where(slot_class[slot] == c, slot_sums[slot], 0.0)
            tile = jnp.where(class_row == c, line, tile)
        totals = jnp.where(class_row == class_lane, jnp.sum(tile, axis=1, keepdims=True), 0.0)
        line = jnp.sum(totals, axis=0, keepdims=True)
        for copy in range(ndp):
            bias_part[ndp * (head_start + head) + copy] = line


def finish_kernel(heads, rows, terms, key_grad, value_grad, bias_grad):
    def total(first, size):
        parts = [terms[i, first : first + size].astype(jnp.float32) for i in range(terms.shape[0])]
        while len(parts) > 1:
            parts = [parts[i] + parts[i + 1] for i in range(0, len(parts), 2)]
        return parts[0]

    for head in range(heads):
        cols = slice(head * HSIZE, (head + 1) * HSIZE)
        key_grad[:, cols] = (total(head * rows, rows) * SCALE).astype(jnp.bfloat16)
        value_grad[:, cols] = total((heads + head) * rows, rows).astype(jnp.bfloat16)
    pieces = jnp.sum(total(2 * heads * rows, RIDE), axis=0, keepdims=True)
    bias_grad[...] = pieces[:, :NREL]


def body(
    query_rows,
    key_rows,
    value_rows,
    summary_keys,
    summary_values,
    out_grad,
    rel_bias,
    pattern,
    block_view,
    summary_view,
):
    tok_rows, width = query_rows.shape[1:]
    heads = width // HSIZE
    nseq = lax.axis_size("seq")
    nfsdp = lax.axis_size("fsdp")
    ndp = lax.axis_size("dp")
    nblk = block_view.shape[1]
    sum_rows = summary_keys.shape[1]
    bf16, f32 = jnp.bfloat16, jnp.float32

    half = nseq // 2
    up = [(i, i + 1) for i in range(nseq - 1) if i + 1 != half]
    down = [(i + 1, i) for i in range(nseq - 1) if i + 1 != half]
    both = ("seq", "dp")

    def spot(row, side, col):
        return (side * half + row) * ndp + col

    last = half - 1
    across = [(spot(last, 0, c), spot(0, 1, c)) for c in range(ndp)]
    across += [(b, a) for a, b in across]
    first_leg, second_leg = [], []
    for side in range(2):
        start, stop = (last, 0) if side == 0 else (0, last)
        for col in range(ndp):
            via = spot(start, side if col else 1 - side, (col - 1) % ndp)
            first_leg.append((spot(start, side, col), via))
            second_leg.append((via, spot(stop, 1 - side, col)))

    table_out = jnp.broadcast_to(rel_bias.reshape(1, NREL), (nfsdp, NREL))
    table = lax.all_to_all(table_out, "fsdp", 0, 0, tiled=True)
    passing = lax.ppermute(value_rows[0], both, first_leg)
    cross_key = lax.ppermute(key_rows[0], both, across)
    own_kv = jnp.concatenate([key_rows[0], value_rows[0]], axis=1)
    left_kv = lax.ppermute(own_kv, "seq", up)
    right_kv = lax.ppermute(own_kv, "seq", down)
    cross_value = lax.ppermute(passing, both, second_leg)
    own_sums = jnp.concatenate([summary_keys[0], summary_values[0]], axis=0)
    sums_out = jnp.broadcast_to(own_sums[None], (nseq, 2 * sum_rows, width))
    sums = lax.all_to_all(sums_out, "seq", 0, 0, tiled=True)
    place = jnp.stack([lax.axis_index("seq"), lax.axis_index("dp") * heads]).astype(jnp.int32)

    smem = pl.BlockSpec(memory_space=pltpu.SMEM)
    vmem = pl.BlockSpec(memory_space=pltpu.VMEM)
    shaped = jax.ShapeDtypeStruct
    attended, query_grad, to_left, to_right, to_cross, own_grad, sum_grad, bias_part = pl.pallas_call(
        functools.partial(attention_kernel, heads, nblk, ndp, half),
        out_shape=(
            shaped((tok_rows, width), bf16),
            shaped((tok_rows, width), bf16),
            shaped((BLK, 2 * width), bf16),
            shaped((BLK, 2 * width), bf16),
            shaped((2, BLK, width), bf16),
            shaped((BLK, 2 * width), f32),
            shaped((nseq, 2 * heads * sum_rows + RIDE, HSIZE), bf16),
            shaped((nfsdp * ndp, 1, BLK), f32),
        ),
        in_specs=[smem] * 4 + [vmem] * 9,
        out_specs=(vmem,) * 8,
        name="attention",
    )(
        place,
        pattern[0],
        block_view[0],
        table,
        summary_view.reshape(-1, 1),
        query_rows[0],
        out_grad[0],
        own_kv,
        left_kv,
        right_kv,
        cross_key,
        cross_value,
        sums,
    )
    bias_part = lax.all_to_all(bias_part, ("fsdp", "dp"), 0, 0, tiled=True)
    passing = lax.ppermute(to_cross[1], both, first_leg)
    from_cross_key = lax.ppermute(to_cross[0], both, across)
    from_right = lax.ppermute(to_left, "seq", down)
    from_left = lax.ppermute(to_right, "seq", up)
    from_cross_value = lax.ppermute(passing, both, second_leg)
    rest = jnp.sum(bias_part, axis=0)
    pieces = []
    for _ in range(3):
        pieces.append(lax.reduce_precision(rest, 8, 7))
        rest = rest - pieces[-1]
    rider = jnp.pad(jnp.concatenate(pieces, axis=0).astype(bf16), ((0, RIDE - 3), (0, 0)))
    rider = jnp.broadcast_to(rider[None], (nseq, RIDE, BLK))
    sum_grad = lax.dynamic_update_slice(sum_grad, rider, (0, 2 * heads * sum_rows, 0))
    sum_terms = lax.all_to_all(sum_grad, "seq", 0, 0, tiled=True)

    grads = own_grad + from_left.astype(f32) + from_right.astype(f32)
    key_grad = ((grads[:, :width] + from_cross_key.astype(f32)) * SCALE).astype(bf16)
    value_grad = (grads[:, width:] + from_cross_value.astype(f32)).astype(bf16)
    summary_key_grad, summary_value_grad, bias_grad = pl.pallas_call(
        functools.partial(finish_kernel, heads, sum_rows),
        out_shape=(
            shaped((sum_rows, width), bf16),
            shaped((sum_rows, width), bf16),
            shaped((1, NREL), f32),
        ),
        in_specs=[vmem],
        out_specs=(vmem,) * 3,
        name="finish",
    )(sum_terms)
    return (
        attended[None],
        query_grad[None],
        key_grad[None],
        value_grad[None],
        summary_key_grad[None],
        summary_value_grad[None],
        bias_grad.reshape(NREL, 1),
    )


def solution(mesh):
    rows = P("fsdp", "seq", "dp")
    return jax.shard_map(
        body,
        mesh=mesh,
        in_specs=(rows,) * 6
        + (P(None, "fsdp"), P("fsdp", None, None), P("fsdp", None), P("fsdp", None)),
        out_specs=(rows,) * 6 + (P(None, "fsdp"),),
        check_vma=False,
    )
```

```python
import functools
import math

import jax
import jax.numpy as jnp
from jax import lax
from jax.experimental import pallas as pl
from jax.experimental.pallas import tpu as pltpu
from jax.sharding import PartitionSpec as P


HSIZE = 128
BLK = 128
NVIEW = 96
NREL = 4
RIDE = 8
NEG_FILL = -1e30
SCALE = 1.0 / math.sqrt(HSIZE)


def view_class(view_a, view_b):
    distance = jnp.abs(view_a - view_b)
    distance = jnp.minimum(distance, NVIEW - distance)
    one = jnp.int32(1)
    zero = jnp.int32(0)
    return (
        jnp.where(distance >= 1, one, zero)
        + jnp.where(distance >= 2, one, zero)
        + jnp.where(distance >= 8, one, zero)
    )


def dot_nt(left, right):
    return lax.dot_general(left, right, (((1,), (1,)), ((), ())), preferred_element_type=jnp.float32)


def dot_nn(left, right):
    return lax.dot_general(left, right, (((1,), (0,)), ((), ())), preferred_element_type=jnp.float32)


def dot_tn(left, right):
    return lax.dot_general(left, right, (((0,), (0,)), ((), ())), preferred_element_type=jnp.float32)


def attention_kernel(
    heads,
    nblk,
    ndp,
    place,
    pattern,
    views,
    table,
    sum_views,
    query,
    grad_out,
    own_kv,
    left_kv,
    right_kv,
    sums,
    attended,
    query_grad,
    to_left,
    to_right,
    own_grad,
    sum_grad,
    bias_part,
):
    block = place[0]
    head_start = place[1]
    own_view = views[block]
    slot_views = [
        views[jnp.maximum(block - 1, 0)],
        own_view,
        views[jnp.minimum(block + 1, nblk - 1)],
    ]
    slot_class = [view_class(own_view, view) for view in slot_views]
    slot_mask = [
        jnp.where(pattern[block, slot] >= 0, jnp.float32(0.0), jnp.float32(NEG_FILL))
        for slot in range(3)
    ]
    sum_class = view_class(own_view, sum_views[...])
    count, rows = sums.shape[0], sums.shape[1] // 2
    bias_part[...] = jnp.zeros_like(bias_part)
    class_row = lax.broadcasted_iota(jnp.int32, (8, BLK), 0)
    class_lane = lax.broadcasted_iota(jnp.int32, (8, BLK), 1)
    for head in range(heads):
        cols = slice(head * HSIZE, (head + 1) * HSIZE)
        late = slice((heads + head) * HSIZE, (heads + head + 1) * HSIZE)
        q = query[:, cols]
        go = grad_out[:, cols]
        keys = jnp.concatenate(
            [
                left_kv[:, cols],
                own_kv[:, cols],
                right_kv[:, cols],
                sums[:, :rows, cols].reshape(count * rows, HSIZE),
            ],
            axis=0,
        )
        values = jnp.concatenate(
            [
                left_kv[:, late],
                own_kv[:, late],
                right_kv[:, late],
                sums[:, rows:, cols].reshape(count * rows, HSIZE),
            ],
            axis=0,
        )
        biases = [table[head_start + head, c] for c in range(NREL)]

        def pick(cls):
            low = jnp.where(cls == 0, biases[0], biases[1])
            high = jnp.where(cls == 2, biases[2], biases[3])
            return jnp.where(cls < 2, low, high)

        raw = dot_nt(keys, q) * SCALE
        scores = jnp.concatenate(
            [
                raw[slot * BLK : (slot + 1) * BLK] + (pick(slot_class[slot]) + slot_mask[slot])
                for slot in range(3)
            ]
            + [raw[3 * BLK :] + pick(sum_class)],
            axis=0,
        )
        row_max = jnp.max(scores, axis=0, keepdims=True)
        lifted = jnp.exp(scores - row_max)
        weights = lifted * (1.0 / jnp.sum(lifted, axis=0, keepdims=True))
        low = weights.astype(jnp.bfloat16)
        prob_grad = dot_nt(values, go)
        row_delta = jnp.sum(weights * prob_grad, axis=0, keepdims=True)
        score_grad = weights * (prob_grad - row_delta)
        grad_low = score_grad.astype(jnp.bfloat16)
        attended[:, cols] = dot_tn(low, values).astype(jnp.bfloat16)
        query_grad[:, cols] = (dot_tn(grad_low, keys) * SCALE).astype(jnp.bfloat16)
        key_terms = dot_nn(grad_low, q)
        value_terms = dot_nn(low, go)
        for index, (terms, where) in enumerate(((key_terms, cols), (value_terms, late))):
            to_left[:, where] = terms[:BLK].astype(jnp.bfloat16)
            own_grad[:, where] = terms[BLK : 2 * BLK]
            to_right[:, where] = terms[2 * BLK : 3 * BLK].astype(jnp.bfloat16)
            first = (index * heads + head) * rows
            sum_grad[:, first : first + rows] = (
                terms[3 * BLK :].astype(jnp.bfloat16).reshape(count, rows, HSIZE)
            )
        slot_sums = [
            jnp.sum(score_grad[slot * BLK : (slot + 1) * BLK], axis=0, keepdims=True)
            for slot in range(3)
        ]
        sum_part = score_grad[3 * BLK :]
        tile = jnp.zeros((8, BLK), jnp.float32)
        for c in range(NREL):
            line = jnp.sum(jnp.where(sum_class == c, sum_part, 0.0), axis=0, keepdims=True)
            for slot in range(3):
                line = line + jnp.where(slot_class[slot] == c, slot_sums[slot], 0.0)
            tile = jnp.where(class_row == c, line, tile)
        totals = jnp.where(class_row == class_lane, jnp.sum(tile, axis=1, keepdims=True), 0.0)
        line = jnp.sum(totals, axis=0, keepdims=True)
        for copy in range(ndp):
            bias_part[ndp * (head_start + head) + copy] = line


def finish_kernel(heads, rows, terms, key_grad, value_grad, bias_grad):
    def total(first, size):
        parts = [terms[i, first : first + size].astype(jnp.float32) for i in range(terms.shape[0])]
        while len(parts) > 1:
            parts = [parts[i] + parts[i + 1] for i in range(0, len(parts), 2)]
        return parts[0]

    for head in range(heads):
        cols = slice(head * HSIZE, (head + 1) * HSIZE)
        key_grad[:, cols] = (total(head * rows, rows) * SCALE).astype(jnp.bfloat16)
        value_grad[:, cols] = total((heads + head) * rows, rows).astype(jnp.bfloat16)
    pieces = jnp.sum(total(2 * heads * rows, RIDE), axis=0, keepdims=True)
    bias_grad[...] = pieces[:, :NREL]


def body(
    query_rows,
    key_rows,
    value_rows,
    summary_keys,
    summary_values,
    out_grad,
    rel_bias,
    pattern,
    block_view,
    summary_view,
):
    tok_rows, width = query_rows.shape[1:]
    heads = width // HSIZE
    nseq = lax.axis_size("seq")
    nfsdp = lax.axis_size("fsdp")
    ndp = lax.axis_size("dp")
    nblk = block_view.shape[1]
    sum_rows = summary_keys.shape[1]
    bf16, f32 = jnp.bfloat16, jnp.float32

    up = [(i, i + 1) for i in range(nseq - 1)]
    down = [(i + 1, i) for i in range(nseq - 1)]
    own_kv = jnp.concatenate([key_rows[0], value_rows[0]], axis=1)
    left_kv = lax.ppermute(own_kv, "seq", up)
    right_kv = lax.ppermute(own_kv, "seq", down)
    own_sums = jnp.concatenate([summary_keys[0], summary_values[0]], axis=0)
    sums_out = jnp.broadcast_to(own_sums[None], (nseq, 2 * sum_rows, width))
    sums = lax.all_to_all(sums_out, "seq", 0, 0, tiled=True)
    row = lax.broadcasted_iota(jnp.int32, (nfsdp, NREL), 0)
    table = jnp.where(row == lax.axis_index("fsdp"), rel_bias.reshape(1, NREL), 0.0)
    for step in range(int(math.log2(nfsdp))):
        other = lax.ppermute(table, "fsdp", [(i, i ^ (1 << step)) for i in range(nfsdp)])
        table = table + other
    place = jnp.stack([lax.axis_index("seq"), lax.axis_index("dp") * heads]).astype(jnp.int32)

    smem = pl.BlockSpec(memory_space=pltpu.SMEM)
    vmem = pl.BlockSpec(memory_space=pltpu.VMEM)
    shaped = jax.ShapeDtypeStruct

    def near(value):
        return pltpu.with_memory_space_constraint(value, pltpu.VMEM)

    attended, query_grad, to_left, to_right, own_grad, sum_grad, bias_part = pl.pallas_call(
        functools.partial(attention_kernel, heads, nblk, ndp),
        out_shape=(
            shaped((tok_rows, width), bf16),
            shaped((tok_rows, width), bf16),
            pltpu.VMEM((BLK, 2 * width), bf16),
            pltpu.VMEM((BLK, 2 * width), bf16),
            pltpu.VMEM((BLK, 2 * width), f32),
            pltpu.VMEM((nseq, 2 * heads * sum_rows + RIDE, HSIZE), bf16),
            pltpu.VMEM((nfsdp * ndp, 1, BLK), f32),
        ),
        in_specs=[smem] * 4 + [vmem] * 7,
        out_specs=(vmem,) * 7,
        compiler_params=pltpu.CompilerParams(vmem_limit_bytes=24 * 2**20),
        name="attention",
    )(
        place,
        pattern[0],
        block_view[0],
        table,
        summary_view.reshape(-1, 1),
        query_rows[0],
        out_grad[0],
        near(own_kv),
        near(left_kv),
        near(right_kv),
        near(sums),
    )
    bias_part = lax.all_to_all(bias_part, ("fsdp", "dp"), 0, 0, tiled=True)
    from_right = lax.ppermute(to_left, "seq", down)
    from_left = lax.ppermute(to_right, "seq", up)
    rest = jnp.sum(bias_part, axis=0)
    pieces = []
    for _ in range(3):
        pieces.append(lax.reduce_precision(rest, 8, 7))
        rest = rest - pieces[-1]
    rider = jnp.pad(jnp.concatenate(pieces, axis=0).astype(bf16), ((0, RIDE - 3), (0, 0)))
    rider = jnp.broadcast_to(rider[None], (nseq, RIDE, BLK))
    sum_grad = lax.dynamic_update_slice(sum_grad, rider, (0, 2 * heads * sum_rows, 0))
    sum_terms = lax.all_to_all(sum_grad, "seq", 0, 0, tiled=True)

    grads = own_grad + from_left.astype(f32) + from_right.astype(f32)
    key_grad = (grads[:, :width] * SCALE).astype(bf16)
    value_grad = grads[:, width:].astype(bf16)
    summary_key_grad, summary_value_grad, bias_grad = pl.pallas_call(
        functools.partial(finish_kernel, heads, sum_rows),
        out_shape=(
            shaped((sum_rows, width), bf16),
            shaped((sum_rows, width), bf16),
            shaped((1, NREL), f32),
        ),
        in_specs=[vmem],
        out_specs=(vmem,) * 3,
        compiler_params=pltpu.CompilerParams(vmem_limit_bytes=16 * 2**20),
        name="finish",
    )(near(sum_terms))
    return (
        attended[None],
        query_grad[None],
        key_grad[None],
        value_grad[None],
        summary_key_grad[None],
        summary_value_grad[None],
        bias_grad.reshape(NREL, 1),
    )


def solution(mesh):
    rows = P("fsdp", "seq", "dp")
    return jax.shard_map(
        body,
        mesh=mesh,
        in_specs=(rows,) * 6
        + (P(None, "fsdp"), P("fsdp", None, None), P("fsdp", None), P("fsdp", None)),
        out_specs=(rows,) * 6 + (P(None, "fsdp"),),
        check_vma=False,
    )
```

```python
import functools
import math

import jax
import jax.numpy as jnp
from jax import lax
from jax.experimental import pallas as pl
from jax.experimental.pallas import tpu as pltpu
from jax.sharding import Mesh
from jax.sharding import PartitionSpec as P


HSIZE = 128
BLK = 128
NVIEW = 96
NREL = 4
RIDE = 8
NEG_FILL = -1e30
SCALE = 1.0 / math.sqrt(HSIZE)


def view_class(view_a, view_b):
    distance = jnp.abs(view_a - view_b)
    distance = jnp.minimum(distance, NVIEW - distance)
    one = jnp.int32(1)
    zero = jnp.int32(0)
    return (
        jnp.where(distance >= 1, one, zero)
        + jnp.where(distance >= 2, one, zero)
        + jnp.where(distance >= 8, one, zero)
    )


def dot_nt(left, right):
    return lax.dot_general(left, right, (((1,), (1,)), ((), ())), preferred_element_type=jnp.float32)


def dot_nn(left, right):
    return lax.dot_general(left, right, (((1,), (0,)), ((), ())), preferred_element_type=jnp.float32)


def dot_tn(left, right):
    return lax.dot_general(left, right, (((0,), (0,)), ((), ())), preferred_element_type=jnp.float32)


def attention_kernel(
    heads,
    nblk,
    nfsdp,
    ndp,
    place,
    pattern,
    views,
    table,
    sum_views,
    query,
    grad_out,
    own_kv,
    left_kv,
    right_kv,
    sums,
    attended,
    query_grad,
    to_left,
    to_right,
    own_grad,
    sum_near,
    sum_far,
    bias_part,
):
    block = place[0]
    head_start = place[1]
    own_view = views[block]
    slot_views = [
        views[jnp.maximum(block - 1, 0)],
        own_view,
        views[jnp.minimum(block + 1, nblk - 1)],
    ]
    slot_class = [view_class(own_view, view) for view in slot_views]
    slot_mask = [
        jnp.where(pattern[block, slot] >= 0, jnp.float32(0.0), jnp.float32(NEG_FILL))
        for slot in range(3)
    ]
    count, rows = sums.shape[0], sums.shape[1] // 4
    part = count * rows
    late_half = block >= nblk // 2
    early_views, late_views = sum_views[:part], sum_views[part:]
    near_views = lax.select(late_half, late_views, early_views)
    far_views = lax.select(late_half, early_views, late_views)
    sum_class = view_class(own_view, jnp.concatenate([near_views, far_views], axis=0))
    bias_part[...] = jnp.zeros_like(bias_part)
    class_row = lax.broadcasted_iota(jnp.int32, (8, BLK), 0)
    class_lane = lax.broadcasted_iota(jnp.int32, (8, BLK), 1)
    for head in range(heads):
        cols = slice(head * HSIZE, (head + 1) * HSIZE)
        late = slice((heads + head) * HSIZE, (heads + head + 1) * HSIZE)
        q = query[:, cols]
        go = grad_out[:, cols]
        keys = jnp.concatenate(
            [
                left_kv[:, cols],
                own_kv[:, cols],
                right_kv[:, cols],
                sums[:, :rows, cols].reshape(part, HSIZE),
                sums[:, 2 * rows : 3 * rows, cols].reshape(part, HSIZE),
            ],
            axis=0,
        )
        values = jnp.concatenate(
            [
                left_kv[:, late],
                own_kv[:, late],
                right_kv[:, late],
                sums[:, rows : 2 * rows, cols].reshape(part, HSIZE),
                sums[:, 3 * rows :, cols].reshape(part, HSIZE),
            ],
            axis=0,
        )
        biases = [table[head_start + head, c] for c in range(NREL)]

        def pick(cls):
            low = jnp.where(cls == 0, biases[0], biases[1])
            high = jnp.where(cls == 2, biases[2], biases[3])
            return jnp.where(cls < 2, low, high)

        raw = dot_nt(keys, q) * SCALE
        scores = jnp.concatenate(
            [
                raw[slot * BLK : (slot + 1) * BLK] + (pick(slot_class[slot]) + slot_mask[slot])
                for slot in range(3)
            ]
            + [raw[3 * BLK :] + pick(sum_class)],
            axis=0,
        )
        row_max = jnp.max(scores, axis=0, keepdims=True)
        lifted = jnp.exp(scores - row_max)
        weights = lifted * (1.0 / jnp.sum(lifted, axis=0, keepdims=True))
        low = weights.astype(jnp.bfloat16)
        prob_grad = dot_nt(values, go)
        row_delta = jnp.sum(weights * prob_grad, axis=0, keepdims=True)
        score_grad = weights * (prob_grad - row_delta)
        grad_low = score_grad.astype(jnp.bfloat16)
        attended[:, cols] = dot_tn(low, values).astype(jnp.bfloat16)
        query_grad[:, cols] = (dot_tn(grad_low, keys) * SCALE).astype(jnp.bfloat16)
        key_terms = dot_nn(grad_low, q)
        value_terms = dot_nn(low, go)
        for index, (terms, where) in enumerate(((key_terms, cols), (value_terms, late))):
            to_left[:, where] = terms[:BLK].astype(jnp.bfloat16)
            own_grad[:, where] = terms[BLK : 2 * BLK]
            to_right[:, where] = terms[2 * BLK : 3 * BLK].astype(jnp.bfloat16)
            first = (index * heads + head) * rows
            near = terms[3 * BLK : 3 * BLK + part]
            far = terms[3 * BLK + part :].astype(jnp.bfloat16)
            sum_near[:, first : first + rows] = near.reshape(count, rows, HSIZE)
            sum_far[:, first : first + rows] = far.reshape(count, rows, HSIZE)
        slot_sums = [
            jnp.sum(score_grad[slot * BLK : (slot + 1) * BLK], axis=0, keepdims=True)
            for slot in range(3)
        ]
        sum_part = score_grad[3 * BLK :]
        tile = jnp.zeros((8, BLK), jnp.float32)
        for c in range(NREL):
            line = jnp.sum(jnp.where(sum_class == c, sum_part, 0.0), axis=0, keepdims=True)
            for slot in range(3):
                line = line + jnp.where(slot_class[slot] == c, slot_sums[slot], 0.0)
            tile = jnp.where(class_row == c, line, tile)
        totals = jnp.where(class_row == class_lane, jnp.sum(tile, axis=1, keepdims=True), 0.0)
        line = jnp.sum(totals, axis=0, keepdims=True)
        for side in range(2):
            for copy in range(ndp):
                bias_part[(side * nfsdp + head_start + head) * ndp + copy] = line


def merge_kernel(near, far, bias_part, merged):
    size = near.shape[1]
    merged[:, :size] = (near[...] + far[...].astype(jnp.float32)).astype(jnp.bfloat16)
    rest = jnp.sum(bias_part[...], axis=0)
    row = lax.broadcasted_iota(jnp.int32, (RIDE, BLK), 0)
    ride = jnp.zeros((RIDE, BLK), jnp.float32)
    for index in range(3):
        piece = rest.astype(jnp.bfloat16).astype(jnp.float32)
        ride = jnp.where(row == index, piece, ride)
        rest = rest - piece
    ride = ride.astype(jnp.bfloat16)
    for i in range(near.shape[0]):
        merged[i, size:] = ride


def finish_kernel(heads, rows, terms, key_grad, value_grad, bias_grad):
    def total(first, size):
        parts = [terms[i, first : first + size].astype(jnp.float32) for i in range(terms.shape[0])]
        while len(parts) > 1:
            parts = [parts[i] + parts[i + 1] for i in range(0, len(parts), 2)]
        return parts[0]

    for head in range(heads):
        cols = slice(head * HSIZE, (head + 1) * HSIZE)
        key_grad[:, cols] = (total(head * rows, rows) * SCALE).astype(jnp.bfloat16)
        value_grad[:, cols] = total((heads + head) * rows, rows).astype(jnp.bfloat16)
    pieces = jnp.sum(total(2 * heads * rows, RIDE), axis=0, keepdims=True)
    bias_grad[...] = pieces[:, :NREL]


def body(
    query_rows,
    key_rows,
    value_rows,
    summary_keys,
    summary_values,
    out_grad,
    rel_bias,
    pattern,
    block_view,
    summary_view,
):
    tok_rows, width = query_rows.shape[1:]
    heads = width // HSIZE
    seq = ("half", "y")
    half = lax.axis_size("y")
    nseq = 2 * half
    nfsdp = lax.axis_size("fsdp")
    ndp = lax.axis_size("dp")
    nblk = block_view.shape[1]
    sum_rows = summary_keys.shape[1]
    bf16, f32 = jnp.bfloat16, jnp.float32

    up = [(i, i + 1) for i in range(nseq - 1)]
    down = [(i + 1, i) for i in range(nseq - 1)]
    swap = [(0, 1), (1, 0)]
    own_kv = jnp.concatenate([key_rows[0], value_rows[0]], axis=1)
    left_kv = lax.ppermute(own_kv, seq, up)
    right_kv = lax.ppermute(own_kv, seq, down)
    table_out = jnp.broadcast_to(rel_bias.reshape(1, NREL), (nfsdp, NREL))
    table = lax.all_to_all(table_out, "fsdp", 0, 0, tiled=True)
    own_sums = jnp.concatenate([summary_keys[0], summary_values[0]], axis=0)
    far_sums = lax.ppermute(own_sums, "half", swap)
    sums_out = jnp.concatenate([own_sums, far_sums], axis=0)
    sums_out = jnp.broadcast_to(sums_out[None], (half, 4 * sum_rows, width))
    sums = lax.all_to_all(sums_out, "y", 0, 0, tiled=True)
    place = jnp.stack([lax.axis_index(seq), lax.axis_index("dp") * heads]).astype(jnp.int32)

    smem = pl.BlockSpec(memory_space=pltpu.SMEM)
    vmem = pl.BlockSpec(memory_space=pltpu.VMEM)
    shaped = jax.ShapeDtypeStruct

    def near(value):
        return pltpu.with_memory_space_constraint(value, pltpu.VMEM)

    attended, query_grad, to_left, to_right, own_grad, near_terms, far_terms, bias_part = pl.pallas_call(
        functools.partial(attention_kernel, heads, nblk, nfsdp, ndp),
        out_shape=(
            shaped((tok_rows, width), bf16),
            shaped((tok_rows, width), bf16),
            shaped((BLK, 2 * width), bf16),
            shaped((BLK, 2 * width), bf16),
            shaped((BLK, 2 * width), f32),
            shaped((half, 2 * heads * sum_rows, HSIZE), f32),
            shaped((half, 2 * heads * sum_rows, HSIZE), bf16),
            shaped((2 * nfsdp * ndp, 1, BLK), f32),
        ),
        in_specs=[smem] * 4 + [vmem] * 7,
        out_specs=(vmem,) * 8,
        compiler_params=pltpu.CompilerParams(vmem_limit_bytes=61 * 2**20),
        name="attention",
    )(
        place,
        pattern[0],
        block_view[0],
        table,
        summary_view.reshape(-1, 1),
        query_rows[0],
        out_grad[0],
        near(own_kv),
        near(left_kv),
        near(right_kv),
        near(sums),
    )
    far_terms = lax.ppermute(far_terms, "half", swap)
    bias_part = lax.all_to_all(bias_part, ("half", "fsdp", "dp"), 0, 0, tiled=True)
    from_right = lax.ppermute(to_left, seq, down)
    from_left = lax.ppermute(to_right, seq, up)
    merged = pl.pallas_call(
        merge_kernel,
        out_shape=shaped((half, 2 * heads * sum_rows + RIDE, HSIZE), bf16),
        in_specs=[vmem] * 3,
        out_specs=vmem,
        compiler_params=pltpu.CompilerParams(vmem_limit_bytes=16 * 2**20),
        name="merge",
    )(near_terms, near(far_terms), near(bias_part))
    sum_terms = lax.all_to_all(merged, "y", 0, 0, tiled=True)

    grads = own_grad + from_left.astype(f32) + from_right.astype(f32)
    key_grad = (grads[:, :width] * SCALE).astype(bf16)
    value_grad = grads[:, width:].astype(bf16)
    summary_key_grad, summary_value_grad, bias_grad = pl.pallas_call(
        functools.partial(finish_kernel, heads, sum_rows),
        out_shape=(
            shaped((sum_rows, width), bf16),
            shaped((sum_rows, width), bf16),
            shaped((1, NREL), f32),
        ),
        in_specs=[vmem],
        out_specs=(vmem,) * 3,
        compiler_params=pltpu.CompilerParams(vmem_limit_bytes=16 * 2**20),
        name="finish",
    )(near(sum_terms))
    return (
        attended[None],
        query_grad[None],
        key_grad[None],
        value_grad[None],
        summary_key_grad[None],
        summary_value_grad[None],
        bias_grad.reshape(NREL, 1),
    )


def solution(mesh):
    nseq, nfsdp, ndp = (mesh.shape[name] for name in ("seq", "fsdp", "dp"))
    split = Mesh(mesh.devices.reshape(2, nseq // 2, nfsdp, ndp), ("half", "y", "fsdp", "dp"))
    rows = P("fsdp", ("half", "y"), "dp")
    return jax.shard_map(
        body,
        mesh=split,
        in_specs=(rows,) * 6
        + (P(None, "fsdp"), P("fsdp", None, None), P("fsdp", None), P("fsdp", None)),
        out_specs=(rows,) * 6 + (P(None, "fsdp"),),
        check_vma=False,
    )
```

```python
import functools
import math

import jax
import jax.numpy as jnp
from jax import lax
from jax.experimental import pallas as pl
from jax.experimental.pallas import tpu as pltpu
from jax.sharding import Mesh
from jax.sharding import PartitionSpec as P


HSIZE = 128
BLK = 128
NVIEW = 96
NREL = 4
RIDE = 8
NEG_FILL = -1e30
SCALE = 1.0 / math.sqrt(HSIZE)


def view_class(view_a, view_b):
    distance = jnp.abs(view_a - view_b)
    distance = jnp.minimum(distance, NVIEW - distance)
    one = jnp.int32(1)
    zero = jnp.int32(0)
    return (
        jnp.where(distance >= 1, one, zero)
        + jnp.where(distance >= 2, one, zero)
        + jnp.where(distance >= 8, one, zero)
    )


def dot_nt(left, right):
    return lax.dot_general(left, right, (((1,), (1,)), ((), ())), preferred_element_type=jnp.float32)


def dot_nn(left, right):
    return lax.dot_general(left, right, (((1,), (0,)), ((), ())), preferred_element_type=jnp.float32)


def dot_tn(left, right):
    return lax.dot_general(left, right, (((0,), (0,)), ((), ())), preferred_element_type=jnp.float32)


def attention_kernel(
    heads,
    nblk,
    nfsdp,
    ndp,
    place,
    pattern,
    views,
    table,
    sum_views,
    query,
    grad_out,
    own_kv,
    left_kv,
    right_kv,
    sums,
    attended,
    query_grad,
    to_left,
    to_right,
    own_grad,
    sum_near,
    sum_far,
    bias_part,
):
    block = place[0]
    head_start = place[1]
    own_view = views[block]
    slot_views = [
        views[jnp.maximum(block - 1, 0)],
        own_view,
        views[jnp.minimum(block + 1, nblk - 1)],
    ]
    slot_class = [view_class(own_view, view) for view in slot_views]
    slot_mask = [
        jnp.where(pattern[block, slot] >= 0, jnp.float32(0.0), jnp.float32(NEG_FILL))
        for slot in range(3)
    ]
    count, rows = sums.shape[0] // 2, sums.shape[1] // 2
    part = count * rows
    late_half = block >= nblk // 2
    near_rows = pl.ds(jnp.where(late_half, count, 0), count)
    far_rows = pl.ds(jnp.where(late_half, 0, count), count)
    early_views, late_views = sum_views[:part], sum_views[part:]
    near_views = lax.select(late_half, late_views, early_views)
    far_views = lax.select(late_half, early_views, late_views)
    sum_class = view_class(own_view, jnp.concatenate([near_views, far_views], axis=0))
    bias_part[...] = jnp.zeros_like(bias_part)
    class_row = lax.broadcasted_iota(jnp.int32, (8, BLK), 0)
    class_lane = lax.broadcasted_iota(jnp.int32, (8, BLK), 1)
    for head in range(heads):
        cols = slice(head * HSIZE, (head + 1) * HSIZE)
        late = slice((heads + head) * HSIZE, (heads + head + 1) * HSIZE)
        q = query[:, cols]
        go = grad_out[:, cols]
        keys = jnp.concatenate(
            [
                left_kv[:, cols],
                own_kv[:, cols],
                right_kv[:, cols],
                sums[near_rows, :rows, cols].reshape(part, HSIZE),
                sums[far_rows, :rows, cols].reshape(part, HSIZE),
            ],
            axis=0,
        )
        values = jnp.concatenate(
            [
                left_kv[:, late],
                own_kv[:, late],
                right_kv[:, late],
                sums[near_rows, rows:, cols].reshape(part, HSIZE),
                sums[far_rows, rows:, cols].reshape(part, HSIZE),
            ],
            axis=0,
        )
        biases = [table[head_start + head, c] for c in range(NREL)]

        def pick(cls):
            low = jnp.where(cls == 0, biases[0], biases[1])
            high = jnp.where(cls == 2, biases[2], biases[3])
            return jnp.where(cls < 2, low, high)

        raw = dot_nt(keys, q) * SCALE
        scores = jnp.concatenate(
            [
                raw[slot * BLK : (slot + 1) * BLK] + (pick(slot_class[slot]) + slot_mask[slot])
                for slot in range(3)
            ]
            + [raw[3 * BLK :] + pick(sum_class)],
            axis=0,
        )
        row_max = jnp.max(scores, axis=0, keepdims=True)
        lifted = jnp.exp(scores - row_max)
        weights = lifted * (1.0 / jnp.sum(lifted, axis=0, keepdims=True))
        low = weights.astype(jnp.bfloat16)
        prob_grad = dot_nt(values, go)
        row_delta = jnp.sum(weights * prob_grad, axis=0, keepdims=True)
        score_grad = weights * (prob_grad - row_delta)
        grad_low = score_grad.astype(jnp.bfloat16)
        attended[:, cols] = dot_tn(low, values).astype(jnp.bfloat16)
        query_grad[:, cols] = (dot_tn(grad_low, keys) * SCALE).astype(jnp.bfloat16)
        key_terms = dot_nn(grad_low, q)
        value_terms = dot_nn(low, go)
        for index, (terms, where) in enumerate(((key_terms, cols), (value_terms, late))):
            to_left[:, where] = terms[:BLK].astype(jnp.bfloat16)
            own_grad[:, where] = terms[BLK : 2 * BLK]
            to_right[:, where] = terms[2 * BLK : 3 * BLK].astype(jnp.bfloat16)
            first = (index * heads + head) * rows
            near = terms[3 * BLK : 3 * BLK + part]
            far = terms[3 * BLK + part :].astype(jnp.bfloat16)
            sum_near[:, first : first + rows] = near.reshape(count, rows, HSIZE)
            sum_far[:, first : first + rows] = far.reshape(count, rows, HSIZE)
        slot_sums = [
            jnp.sum(score_grad[slot * BLK : (slot + 1) * BLK], axis=0, keepdims=True)
            for slot in range(3)
        ]
        sum_part = score_grad[3 * BLK :]
        tile = jnp.zeros((8, BLK), jnp.float32)
        for c in range(NREL):
            line = jnp.sum(jnp.where(sum_class == c, sum_part, 0.0), axis=0, keepdims=True)
            for slot in range(3):
                line = line + jnp.where(slot_class[slot] == c, slot_sums[slot], 0.0)
            tile = jnp.where(class_row == c, line, tile)
        totals = jnp.where(class_row == class_lane, jnp.sum(tile, axis=1, keepdims=True), 0.0)
        line = jnp.sum(totals, axis=0, keepdims=True)
        for side in range(2):
            for copy in range(ndp):
                bias_part[(side * nfsdp + head_start + head) * ndp + copy] = line


def merge_kernel(near, far, bias_part, merged):
    size = near.shape[1]
    merged[:, :size] = (near[...] + far[...].astype(jnp.float32)).astype(jnp.bfloat16)
    rest = jnp.sum(bias_part[...], axis=0)
    row = lax.broadcasted_iota(jnp.int32, (RIDE, BLK), 0)
    ride = jnp.zeros((RIDE, BLK), jnp.float32)
    for index in range(3):
        piece = rest.astype(jnp.bfloat16).astype(jnp.float32)
        ride = jnp.where(row == index, piece, ride)
        rest = rest - piece
    ride = ride.astype(jnp.bfloat16)
    for i in range(near.shape[0]):
        merged[i, size:] = ride


def finish_kernel(heads, rows, terms, key_grad, value_grad, bias_grad):
    def total(first, size):
        parts = [terms[i, first : first + size].astype(jnp.float32) for i in range(terms.shape[0])]
        while len(parts) > 1:
            parts = [parts[i] + parts[i + 1] for i in range(0, len(parts), 2)]
        return parts[0]

    for head in range(heads):
        cols = slice(head * HSIZE, (head + 1) * HSIZE)
        key_grad[:, cols] = (total(head * rows, rows) * SCALE).astype(jnp.bfloat16)
        value_grad[:, cols] = total((heads + head) * rows, rows).astype(jnp.bfloat16)
    pieces = jnp.sum(total(2 * heads * rows, RIDE), axis=0, keepdims=True)
    bias_grad[...] = pieces[:, :NREL]


def body(
    query_rows,
    key_rows,
    value_rows,
    summary_keys,
    summary_values,
    out_grad,
    rel_bias,
    pattern,
    block_view,
    summary_view,
):
    tok_rows, width = query_rows.shape[1:]
    heads = width // HSIZE
    seq = ("half", "y")
    half = lax.axis_size("y")
    nseq = 2 * half
    nfsdp = lax.axis_size("fsdp")
    ndp = lax.axis_size("dp")
    nblk = block_view.shape[1]
    sum_rows = summary_keys.shape[1]
    bf16, f32 = jnp.bfloat16, jnp.float32

    up = [(i, i + 1) for i in range(nseq - 1)]
    down = [(i + 1, i) for i in range(nseq - 1)]
    swap = [(0, 1), (1, 0)]
    own_kv = jnp.concatenate([key_rows[0], value_rows[0]], axis=1)
    left_kv = lax.ppermute(own_kv, seq, up)
    right_kv = lax.ppermute(own_kv, seq, down)
    own_sums = jnp.concatenate([summary_keys[0], summary_values[0]], axis=0)
    sums_out = jnp.broadcast_to(own_sums[None], (nseq, 2 * sum_rows, width))
    sums = lax.all_to_all(sums_out, seq, 0, 0, tiled=True)
    row = lax.broadcasted_iota(jnp.int32, (nfsdp, NREL), 0)
    table = jnp.where(row == lax.axis_index("fsdp"), rel_bias.reshape(1, NREL), 0.0)
    for step in range(int(math.log2(nfsdp))):
        other = lax.ppermute(table, "fsdp", [(i, i ^ (1 << step)) for i in range(nfsdp)])
        table = table + other
    place = jnp.stack([lax.axis_index(seq), lax.axis_index("dp") * heads]).astype(jnp.int32)

    smem = pl.BlockSpec(memory_space=pltpu.SMEM)
    vmem = pl.BlockSpec(memory_space=pltpu.VMEM)
    shaped = jax.ShapeDtypeStruct

    def near(value):
        return pltpu.with_memory_space_constraint(value, pltpu.VMEM)

    attended, query_grad, to_left, to_right, own_grad, near_terms, far_terms, bias_part = pl.pallas_call(
        functools.partial(attention_kernel, heads, nblk, nfsdp, ndp),
        out_shape=(
            shaped((tok_rows, width), bf16),
            shaped((tok_rows, width), bf16),
            shaped((BLK, 2 * width), bf16),
            shaped((BLK, 2 * width), bf16),
            shaped((BLK, 2 * width), f32),
            shaped((half, 2 * heads * sum_rows, HSIZE), f32),
            shaped((half, 2 * heads * sum_rows, HSIZE), bf16),
            shaped((2 * nfsdp * ndp, 1, BLK), f32),
        ),
        in_specs=[smem] * 4 + [vmem] * 7,
        out_specs=(vmem,) * 8,
        compiler_params=pltpu.CompilerParams(vmem_limit_bytes=61 * 2**20),
        name="attention",
    )(
        place,
        pattern[0],
        block_view[0],
        table,
        summary_view.reshape(-1, 1),
        query_rows[0],
        out_grad[0],
        near(own_kv),
        near(left_kv),
        near(right_kv),
        near(sums),
    )
    far_terms = lax.ppermute(far_terms, "half", swap)
    bias_part = lax.all_to_all(bias_part, ("half", "fsdp", "dp"), 0, 0, tiled=True)
    from_right = lax.ppermute(to_left, seq, down)
    from_left = lax.ppermute(to_right, seq, up)
    merged = pl.pallas_call(
        merge_kernel,
        out_shape=shaped((half, 2 * heads * sum_rows + RIDE, HSIZE), bf16),
        in_specs=[vmem] * 3,
        out_specs=vmem,
        compiler_params=pltpu.CompilerParams(vmem_limit_bytes=16 * 2**20),
        name="merge",
    )(near_terms, near(far_terms), near(bias_part))
    sum_terms = lax.all_to_all(merged, "y", 0, 0, tiled=True)

    grads = own_grad + from_left.astype(f32) + from_right.astype(f32)
    key_grad = (grads[:, :width] * SCALE).astype(bf16)
    value_grad = grads[:, width:].astype(bf16)
    summary_key_grad, summary_value_grad, bias_grad = pl.pallas_call(
        functools.partial(finish_kernel, heads, sum_rows),
        out_shape=(
            shaped((sum_rows, width), bf16),
            shaped((sum_rows, width), bf16),
            shaped((1, NREL), f32),
        ),
        in_specs=[vmem],
        out_specs=(vmem,) * 3,
        compiler_params=pltpu.CompilerParams(vmem_limit_bytes=16 * 2**20),
        name="finish",
    )(near(sum_terms))
    return (
        attended[None],
        query_grad[None],
        key_grad[None],
        value_grad[None],
        summary_key_grad[None],
        summary_value_grad[None],
        bias_grad.reshape(NREL, 1),
    )


def solution(mesh):
    nseq, nfsdp, ndp = (mesh.shape[name] for name in ("seq", "fsdp", "dp"))
    split = Mesh(mesh.devices.reshape(2, nseq // 2, nfsdp, ndp), ("half", "y", "fsdp", "dp"))
    rows = P("fsdp", ("half", "y"), "dp")
    return jax.shard_map(
        body,
        mesh=split,
        in_specs=(rows,) * 6
        + (P(None, "fsdp"), P("fsdp", None, None), P("fsdp", None), P("fsdp", None)),
        out_specs=(rows,) * 6 + (P(None, "fsdp"),),
        check_vma=False,
    )
```

```python
import functools
import math

import jax
import jax.numpy as jnp
from jax import lax
from jax.experimental import pallas as pl
from jax.experimental.pallas import tpu as pltpu
from jax.sharding import Mesh
from jax.sharding import PartitionSpec as P


HSIZE = 128
BLK = 128
NVIEW = 96
NREL = 4
RIDE = 8
NEG_FILL = -1e30
SCALE = 1.0 / math.sqrt(HSIZE)


def view_class(view_a, view_b):
    distance = jnp.abs(view_a - view_b)
    distance = jnp.minimum(distance, NVIEW - distance)
    one = jnp.int32(1)
    zero = jnp.int32(0)
    return (
        jnp.where(distance >= 1, one, zero)
        + jnp.where(distance >= 2, one, zero)
        + jnp.where(distance >= 8, one, zero)
    )


def dot_nt(left, right):
    return lax.dot_general(left, right, (((1,), (1,)), ((), ())), preferred_element_type=jnp.float32)


def dot_nn(left, right):
    return lax.dot_general(left, right, (((1,), (0,)), ((), ())), preferred_element_type=jnp.float32)


def dot_tn(left, right):
    return lax.dot_general(left, right, (((0,), (0,)), ((), ())), preferred_element_type=jnp.float32)


def attention_kernel(
    heads,
    nblk,
    nfsdp,
    ndp,
    place,
    pattern,
    views,
    table,
    sum_views,
    query,
    grad_out,
    own_kv,
    left_kv,
    right_kv,
    sums,
    attended,
    query_grad,
    to_left,
    to_right,
    own_grad,
    sum_near,
    sum_far,
    bias_part,
):
    block = place[0]
    head_start = place[1]
    own_view = views[block]
    slot_views = [
        views[jnp.maximum(block - 1, 0)],
        own_view,
        views[jnp.minimum(block + 1, nblk - 1)],
    ]
    slot_class = [view_class(own_view, view) for view in slot_views]
    slot_mask = [
        jnp.where(pattern[block, slot] >= 0, jnp.float32(0.0), jnp.float32(NEG_FILL))
        for slot in range(3)
    ]
    count, rows = sums.shape[0] // 2, sums.shape[1] // 2
    part = count * rows
    late_half = block >= nblk // 2
    near_rows = pl.ds(jnp.where(late_half, count, 0), count)
    far_rows = pl.ds(jnp.where(late_half, 0, count), count)
    early_views, late_views = sum_views[:part], sum_views[part:]
    near_views = lax.select(late_half, late_views, early_views)
    far_views = lax.select(late_half, early_views, late_views)
    sum_class = view_class(own_view, jnp.concatenate([near_views, far_views], axis=0))
    bias_part[...] = jnp.zeros_like(bias_part)
    class_row = lax.broadcasted_iota(jnp.int32, (8, BLK), 0)
    class_lane = lax.broadcasted_iota(jnp.int32, (8, BLK), 1)
    for head in range(heads):
        cols = slice(head * HSIZE, (head + 1) * HSIZE)
        late = slice((heads + head) * HSIZE, (heads + head + 1) * HSIZE)
        q = query[:, cols]
        go = grad_out[:, cols]
        keys = jnp.concatenate(
            [
                left_kv[:, cols],
                own_kv[:, cols],
                right_kv[:, cols],
                sums[near_rows, :rows, cols].reshape(part, HSIZE),
                sums[far_rows, :rows, cols].reshape(part, HSIZE),
            ],
            axis=0,
        )
        values = jnp.concatenate(
            [
                left_kv[:, late],
                own_kv[:, late],
                right_kv[:, late],
                sums[near_rows, rows:, cols].reshape(part, HSIZE),
                sums[far_rows, rows:, cols].reshape(part, HSIZE),
            ],
            axis=0,
        )
        biases = [table[head_start + head, c] for c in range(NREL)]

        def pick(cls):
            low = jnp.where(cls == 0, biases[0], biases[1])
            high = jnp.where(cls == 2, biases[2], biases[3])
            return jnp.where(cls < 2, low, high)

        raw = dot_nt(keys, q) * SCALE
        scores = jnp.concatenate(
            [
                raw[slot * BLK : (slot + 1) * BLK] + (pick(slot_class[slot]) + slot_mask[slot])
                for slot in range(3)
            ]
            + [raw[3 * BLK :] + pick(sum_class)],
            axis=0,
        )
        row_max = jnp.max(scores, axis=0, keepdims=True)
        lifted = jnp.exp(scores - row_max)
        weights = lifted * (1.0 / jnp.sum(lifted, axis=0, keepdims=True))
        low = weights.astype(jnp.bfloat16)
        prob_grad = dot_nt(values, go)
        row_delta = jnp.sum(weights * prob_grad, axis=0, keepdims=True)
        score_grad = weights * (prob_grad - row_delta)
        grad_low = score_grad.astype(jnp.bfloat16)
        attended[:, cols] = dot_tn(low, values).astype(jnp.bfloat16)
        query_grad[:, cols] = (dot_tn(grad_low, keys) * SCALE).astype(jnp.bfloat16)
        key_terms = dot_nn(grad_low, q)
        value_terms = dot_nn(low, go)
        for index, (terms, where) in enumerate(((key_terms, cols), (value_terms, late))):
            to_left[:, where] = terms[:BLK].astype(jnp.bfloat16)
            own_grad[:, where] = terms[BLK : 2 * BLK]
            to_right[:, where] = terms[2 * BLK : 3 * BLK].astype(jnp.bfloat16)
            first = (index * heads + head) * rows
            near = terms[3 * BLK : 3 * BLK + part]
            far = terms[3 * BLK + part :].astype(jnp.bfloat16)
            sum_near[:, first : first + rows] = near.reshape(count, rows, HSIZE)
            sum_far[:, first : first + rows] = far.reshape(count, rows, HSIZE)
        slot_sums = [
            jnp.sum(score_grad[slot * BLK : (slot + 1) * BLK], axis=0, keepdims=True)
            for slot in range(3)
        ]
        sum_part = score_grad[3 * BLK :]
        tile = jnp.zeros((8, BLK), jnp.float32)
        for c in range(NREL):
            line = jnp.sum(jnp.where(sum_class == c, sum_part, 0.0), axis=0, keepdims=True)
            for slot in range(3):
                line = line + jnp.where(slot_class[slot] == c, slot_sums[slot], 0.0)
            tile = jnp.where(class_row == c, line, tile)
        totals = jnp.where(class_row == class_lane, jnp.sum(tile, axis=1, keepdims=True), 0.0)
        line = jnp.sum(totals, axis=0, keepdims=True)
        for side in range(2):
            for copy in range(ndp):
                bias_part[(side * nfsdp + head_start + head) * ndp + copy] = line


def merge_kernel(near, far, bias_part, merged):
    size = near.shape[1]
    merged[:, :size] = (near[...] + far[...].astype(jnp.float32)).astype(jnp.bfloat16)
    rest = jnp.sum(bias_part[...], axis=0)
    row = lax.broadcasted_iota(jnp.int32, (RIDE, BLK), 0)
    ride = jnp.zeros((RIDE, BLK), jnp.float32)
    for index in range(3):
        piece = rest.astype(jnp.bfloat16).astype(jnp.float32)
        ride = jnp.where(row == index, piece, ride)
        rest = rest - piece
    ride = ride.astype(jnp.bfloat16)
    for i in range(near.shape[0]):
        merged[i, size:] = ride


def finish_kernel(heads, rows, terms, key_grad, value_grad, bias_grad):
    def total(first, size):
        parts = [terms[i, first : first + size].astype(jnp.float32) for i in range(terms.shape[0])]
        while len(parts) > 1:
            parts = [parts[i] + parts[i + 1] for i in range(0, len(parts), 2)]
        return parts[0]

    for head in range(heads):
        cols = slice(head * HSIZE, (head + 1) * HSIZE)
        key_grad[:, cols] = (total(head * rows, rows) * SCALE).astype(jnp.bfloat16)
        value_grad[:, cols] = total((heads + head) * rows, rows).astype(jnp.bfloat16)
    pieces = jnp.sum(total(2 * heads * rows, RIDE), axis=0, keepdims=True)
    bias_grad[...] = pieces[:, :NREL]


def body(
    query_rows,
    key_rows,
    value_rows,
    summary_keys,
    summary_values,
    out_grad,
    rel_bias,
    pattern,
    block_view,
    summary_view,
):
    tok_rows, width = query_rows.shape[1:]
    heads = width // HSIZE
    seq = ("half", "y")
    half = lax.axis_size("y")
    nseq = 2 * half
    nfsdp = lax.axis_size("fsdp")
    ndp = lax.axis_size("dp")
    nblk = block_view.shape[1]
    sum_rows = summary_keys.shape[1]
    bf16, f32 = jnp.bfloat16, jnp.float32

    up = [(i, i + 1) for i in range(nseq - 1)]
    down = [(i + 1, i) for i in range(nseq - 1)]
    swap = [(0, 1), (1, 0)]
    own_kv = jnp.concatenate([key_rows[0], value_rows[0]], axis=1)
    left_kv = lax.ppermute(own_kv, seq, up)
    right_kv = lax.ppermute(own_kv, seq, down)
    own_sums = jnp.concatenate([summary_keys[0], summary_values[0]], axis=0)
    sums_out = jnp.broadcast_to(own_sums[None], (nseq, 2 * sum_rows, width))
    sums = lax.all_to_all(sums_out, seq, 0, 0, tiled=True)
    row = lax.broadcasted_iota(jnp.int32, (nfsdp, NREL), 0)
    table = jnp.where(row == lax.axis_index("fsdp"), rel_bias.reshape(1, NREL), 0.0)
    bits = list(range(int(math.log2(nfsdp))))
    bits.insert(1, bits.pop())
    for bit in bits:
        other = lax.ppermute(table, "fsdp", [(i, i ^ (1 << bit)) for i in range(nfsdp)])
        table = table + other
    place = jnp.stack([lax.axis_index(seq), lax.axis_index("dp") * heads]).astype(jnp.int32)

    smem = pl.BlockSpec(memory_space=pltpu.SMEM)
    vmem = pl.BlockSpec(memory_space=pltpu.VMEM)
    shaped = jax.ShapeDtypeStruct

    def near(value):
        return pltpu.with_memory_space_constraint(value, pltpu.VMEM)

    attended, query_grad, to_left, to_right, own_grad, near_terms, far_terms, bias_part = pl.pallas_call(
        functools.partial(attention_kernel, heads, nblk, nfsdp, ndp),
        out_shape=(
            shaped((tok_rows, width), bf16),
            shaped((tok_rows, width), bf16),
            shaped((BLK, 2 * width), bf16),
            shaped((BLK, 2 * width), bf16),
            shaped((BLK, 2 * width), f32),
            shaped((half, 2 * heads * sum_rows, HSIZE), f32),
            shaped((half, 2 * heads * sum_rows, HSIZE), bf16),
            shaped((2 * nfsdp * ndp, 1, BLK), f32),
        ),
        in_specs=[smem] * 4 + [vmem] * 7,
        out_specs=(vmem,) * 8,
        compiler_params=pltpu.CompilerParams(vmem_limit_bytes=61 * 2**20),
        name="attention",
    )(
        place,
        pattern[0],
        block_view[0],
        table,
        summary_view.reshape(-1, 1),
        query_rows[0],
        out_grad[0],
        near(own_kv),
        near(left_kv),
        near(right_kv),
        near(sums),
    )
    far_terms = lax.ppermute(far_terms, "half", swap)
    bias_part = lax.all_to_all(bias_part, ("half", "fsdp", "dp"), 0, 0, tiled=True)
    from_right = lax.ppermute(to_left, seq, down)
    from_left = lax.ppermute(to_right, seq, up)
    merged = pl.pallas_call(
        merge_kernel,
        out_shape=shaped((half, 2 * heads * sum_rows + RIDE, HSIZE), bf16),
        in_specs=[vmem] * 3,
        out_specs=vmem,
        compiler_params=pltpu.CompilerParams(vmem_limit_bytes=16 * 2**20),
        name="merge",
    )(near_terms, near(far_terms), near(bias_part))
    sum_terms = lax.all_to_all(merged, "y", 0, 0, tiled=True)

    grads = own_grad + from_left.astype(f32) + from_right.astype(f32)
    key_grad = (grads[:, :width] * SCALE).astype(bf16)
    value_grad = grads[:, width:].astype(bf16)
    summary_key_grad, summary_value_grad, bias_grad = pl.pallas_call(
        functools.partial(finish_kernel, heads, sum_rows),
        out_shape=(
            shaped((sum_rows, width), bf16),
            shaped((sum_rows, width), bf16),
            shaped((1, NREL), f32),
        ),
        in_specs=[vmem],
        out_specs=(vmem,) * 3,
        compiler_params=pltpu.CompilerParams(vmem_limit_bytes=16 * 2**20),
        name="finish",
    )(near(sum_terms))
    return (
        attended[None],
        query_grad[None],
        key_grad[None],
        value_grad[None],
        summary_key_grad[None],
        summary_value_grad[None],
        bias_grad.reshape(NREL, 1),
    )


def solution(mesh):
    nseq, nfsdp, ndp = (mesh.shape[name] for name in ("seq", "fsdp", "dp"))
    split = Mesh(mesh.devices.reshape(2, nseq // 2, nfsdp, ndp), ("half", "y", "fsdp", "dp"))
    rows = P("fsdp", ("half", "y"), "dp")
    return jax.shard_map(
        body,
        mesh=split,
        in_specs=(rows,) * 6
        + (P(None, "fsdp"), P("fsdp", None, None), P("fsdp", None), P("fsdp", None)),
        out_specs=(rows,) * 6 + (P(None, "fsdp"),),
        check_vma=False,
    )
```
